128 devices in a mesh: lat: 8 (over z, core), lon: 16 (over y, x).
Axes of the slice: x: 4, y: 4, z: 4, core: 2. Of those that a mesh axis runs over, the one named last changes fastest.
Arguments:
- winds: bfloat16 [32, 64, 3, 40, 128], P('lat', 'lon'), may hold values from -6 to 6
- positions: float32 [16384, 3, 128], P(('lat', 'lon')), may hold values from 0 to 39, as said below
- velocity: float32 [16384, 3, 128], P(('lat', 'lon')), may hold values from -6 to 6
- increments: float32 [16384, 3, 128], P(('lat', 'lon')), may hold values from -6 to 6
- mass: float32 [16384, 8, 128], P(('lat', 'lon')), may hold values from 0.1 to 1
- requests: int32 [128, 128, 2], P(('lat', 'lon')), may hold values from 0 to 15
- block_slots: int32 [16384, 1], P(('lat', 'lon')), may hold values from 0 to 255; in each aligned block of 128 rows (0 to 127, 128 to 255, ...) at most 2 rows name the same one
- destinations: int32 [16384, 1], P(('lat', 'lon')), may hold values from 0 to 127; in each aligned block of 128 rows (0 to 127, 128 to 255, ...) at most 2 rows name the same one
- cell_keys: int32 [16384, 128], P(('lat', 'lon')), may hold values from 0 to 2047, as said below
Outputs:
- moved: float32 [16384, 3, 128], P(('lat', 'lon'))
- turbulence: float32 [16384, 3, 128], P(('lat', 'lon'))
- concentration: float32 [32, 64, 8, 40, 128], P('lat', 'lon')
The draws below stay inside these ranges and needn't reach their ends.
Inputs may be any that keep to these rules, and one draw needn't show every extreme that they name: `positions`: component 0 (cell row) lies in 0 to 7, component 1 (cell column) in 0 to 15, component 2 (level) in 0 to 39. requests[o, t, k] names a met block of tile t by its local number. `block_slots`: slot k stands for the (k % 2)-th request that the owner sends to tile k // 2; of the 128 blocks of one owner at most 2 have the same slot, and on some owners one slot gets exactly 2. `destinations`: of the 128 blocks of one owner at most 2 have the same destination; on some owners one destination gets exactly 2. `cell_keys`: a key is (local met block) * 128 + cell of the destination tile; all keys of one particle block lie in one met block.
All inputs are finite; a program needn't handle non-finite values.
Results may differ from the reference program's by a relative error of at most 0.0027.
Values may be sent and summed in bfloat16 or wider, within the bound.
No kernel may reach another device: no remote copies, remote signals or barrier semaphores. Data moves between devices by JAX's collectives and lax.ppermute only.
A program may use at most 64 MiB of HBM per device.

```python
import math
import jax
import jax.numpy as jnp
import numpy as np
from jax import lax

BY = 8
BX = 16
MBC = 128
LEV = 40
S = 8
BLK = 128
MBR = 4
MBK = 4
MB = 16
Q = 2
PB = 128
CAP = 2
BLOCKS = 16384
N_LAT = 8
N_LON = 16
DEVICES = 128


def draw_positions(key, part):
    unit = jax.random.uniform(jax.random.fold_in(key, 11), (BLOCKS, 3, BLK), jnp.float32)
    upper = jnp.array([BY - 1, BX - 1, LEV - 1], jnp.float32)
    return unit * upper[None, :, None]


def draw_cell_keys(key, part):
    first, second = jax.random.split(jax.random.fold_in(key, 7))
    home = jax.random.randint(first, (BLOCKS, 1), 0, MBR * MBK)
    inside = jax.random.randint(second, (BLOCKS, BLK), 0, MBC)
    return (home * MBC + inside).astype(jnp.int32)


def plant(drawn, rng, least, largest):
    index_at = [jax.random.randint(jax.random.fold_in(rng, axis), (), 0, length) for axis, length in enumerate(drawn.shape)]
    longest = drawn.shape.index(max(drawn.shape))
    neighbour = index_at[:longest] + [(index_at[longest] + 1) % drawn.shape[longest]] + index_at[longest + 1:]
    return drawn.at[tuple(index_at)].set(least).at[tuple(neighbour)].set(largest)


def block_levels(rng, shape, pieces, low, top_value):
    def one(dim, parts):
        heights = jax.random.uniform(jax.random.fold_in(jax.random.fold_in(rng, 6), dim), (parts,), jnp.float32, low / len(pieces), top_value / len(pieces))
        return jnp.repeat(jnp.exp(heights), shape[dim] // parts).reshape((-1,) + (1,) * (len(shape) - dim - 1))

    gain = one(*pieces[0])
    for cut in pieces[1:]:
        gain = gain * one(*cut)
    return gain


def shared_out(own_key, own, number, rows, count, top, most, lean):
    order = jax.random.permutation(own_key, count)
    heavy_load, ordinary = load_shares(count, rows * top, most, lean, True), load_shares(count, rows * top, most, lean, False)
    places = jnp.arange(count)

    def named(lengths, rotation):
        used = int((lengths > 0).sum())
        fixed = max(1, used // 4)
        shifted = fixed + (places - fixed + rotation * (used - fixed)) % max(1, count - fixed)
        return jnp.zeros((count,), jnp.int32).at[order[jnp.where(places < fixed, places, shifted)]].set(jnp.asarray(lengths, jnp.int32))

    lengths = jnp.where(number % 4 == 0, named(heavy_load, number // 4), named(ordinary, number - number // 4 - 1))
    mixed = jax.random.permutation(jax.random.fold_in(own, 3), count)
    donor, sink = mixed[0:count // 2 * 2:2], mixed[1:count // 2 * 2:2]
    margin = jnp.minimum(lengths[donor] - 1, most - lengths[sink]) // 2
    margin = jnp.where((donor == order[0]) | (sink == order[0]) | (lengths[sink] == 0), 0, jnp.maximum(margin, 0))
    shifted = jax.random.randint(jax.random.fold_in(own, 4), (count // 2,), 0, 1 << 20) % (margin + 1)
    lengths = lengths.at[donor].add(-shifted).at[sink].add(shifted)
    items = jnp.searchsorted(jnp.cumsum(lengths), jnp.arange(rows * top), side="right").astype(jnp.int32)
    grid = items.reshape(top, rows).T
    grid = grid[jax.random.permutation(jax.random.fold_in(own, 1), rows)]
    rotation = jax.random.randint(jax.random.fold_in(own, 2), (rows, 1), 0, top)
    return jnp.take_along_axis(grid, (jnp.arange(top)[None, :] + rotation) % top, axis=1)


def load_shares(count, total, limit, skew, full):
    weights = [(1 << 20) // math.isqrt(grade ** skew) + 1 for grade in range(1, count + 1)]
    largest = limit if full else min(limit, max(-(-total // count), total * weights[0] // sum(weights)))
    least = 1 if total - largest >= count - 1 else 0
    counts, rest = [largest] + [least] * (count - 1), total - largest - least * (count - 1)
    while rest > 0:
        free = [i for i in range(1, count) if counts[i] < largest] or [i for i in range(1, count) if counts[i] < limit]
        whole, budget = sum([weights[i] for i in free]), rest
        for i in free:
            addition = min(limit - counts[i], max(1, budget * weights[i] // whole), rest)
            counts[i] = counts[i] + addition
            rest = rest - addition
    return np.array(counts)


def normal_values(stream_key, extent, deviation, limit, pieces=(), kind=jnp.bfloat16):
    gain = block_levels(stream_key, extent, pieces, -0.22, 0.18) if pieces else 1.0
    values = jax.random.normal(stream_key, extent, jnp.float32) * deviation * gain
    return jnp.minimum(jnp.maximum(values, -limit), limit).astype(kind)


def setup_inputs(seed: int = 0) -> dict:
    streams_of = jax.random.split(jax.random.key(seed), 10)
    winds = normal_values(streams_of[0], (MBR * N_LAT, MBK * N_LON, 3, LEV, MBC), 1.0, 6.0, ((0, 8), (1, 16)))
    positions = draw_positions(jax.random.fold_in(streams_of[9], 71), 0)
    velocity = normal_values(streams_of[2], (BLOCKS, 3, BLK), 1.0, 6.0, ((0, 128),), jnp.float32)
    increments = normal_values(streams_of[3], (BLOCKS, 3, BLK), 1.0, 6.0, ((0, 128),), jnp.float32)
    mass = jnp.clip(jnp.exp(math.log(1.0) - 2.3025851 * jax.random.uniform(streams_of[4], (BLOCKS, S, BLK), jnp.float32) ** block_levels(streams_of[4], (BLOCKS, S, BLK), ((0, 128),), -0.2, 0.2)), 0.1, 1.0)
    requests = plant(jax.random.randint(streams_of[5], (DEVICES, DEVICES, Q), 0, MB), jax.random.fold_in(streams_of[5], 1), 0, MB - 1).astype(jnp.int32)
    block_slots_keys = jax.random.split(jax.random.fold_in(streams_of[6], 1), BLOCKS // PB)
    block_slots_turns = jax.random.permutation(jax.random.fold_in(streams_of[6], 3), BLOCKS // PB)
    block_slots = jax.vmap(lambda own, number: shared_out(jax.random.fold_in(streams_of[6], 2), own, number, PB, DEVICES * Q, 1, CAP, 2))(block_slots_keys, block_slots_turns).reshape((BLOCKS, 1))
    destinations_keys = jax.random.split(jax.random.fold_in(streams_of[7], 1), BLOCKS // PB)
    destinations_turns = jax.random.permutation(jax.random.fold_in(streams_of[7], 3), BLOCKS // PB)
    destinations = jax.vmap(lambda own, number: shared_out(jax.random.fold_in(streams_of[7], 2), own, number, PB, DEVICES, 1, CAP, 2))(destinations_keys, destinations_turns).reshape((BLOCKS, 1))
    cell_keys = draw_cell_keys(jax.random.fold_in(streams_of[9], 71), 0)
    return dict(winds=winds, positions=positions, velocity=velocity, increments=increments, mass=mass, requests=requests, block_slots=block_slots, destinations=destinations, cell_keys=cell_keys)


DECAY = 0.8
KICK = 0.6
STEP = 0.5


def corner(coord, top):
    base = jnp.clip(jnp.floor(coord), 0, top - 1).astype(jnp.int32)
    frac = coord - base.astype(coord.dtype)
    return base, frac


def reference(winds, positions, velocity, increments, mass, requests, block_slots, destinations, cell_keys):
    devices = N_LAT * N_LON
    block_cols = MBK * N_LON
    table = winds.reshape(-1)
    conc = jnp.zeros((MBR * N_LAT * block_cols * S * LEV * MBC,), jnp.float32)
    upper = jnp.array([BY - 1, BX - 1, LEV - 1], jnp.float32)

    def owner_step(total, items):
        pos, vel, noise, share, asked, slots, target, keys = items
        source = slots // Q
        local = asked[source, slots % Q]
        grow = (source // N_LON) * MBR + local // MBK
        gcol = (source % N_LON) * MBK + local % MBK
        blockid = (grow * block_cols + gcol)[:, None]
        row0, fy = corner(pos[:, 0], BY - 1)
        col0, fx = corner(pos[:, 1], BX - 1)
        lev0, fz = corner(pos[:, 2], LEV - 1)
        wz0 = (1.0 - fz).astype(jnp.bfloat16).astype(jnp.float32)
        wz1 = fz.astype(jnp.bfloat16).astype(jnp.float32)
        winds_at = []
        for comp in range(3):
            acc = jnp.zeros(fy.shape, jnp.float32)
            for di in range(2):
                hy = (1.0 - fy) if di == 0 else fy
                for dj in range(2):
                    hx = (1.0 - fx) if dj == 0 else fx
                    cell = (row0 + di) * BX + col0 + dj
                    base = (blockid * 3 + comp) * LEV
                    low = table[(base + lev0) * MBC + cell].astype(jnp.float32)
                    high = table[(base + lev0 + 1) * MBC + cell].astype(jnp.float32)
                    acc = acc + (hy * hx) * (wz0 * low + wz1 * high)
            winds_at.append(acc)
        wind = jnp.stack(winds_at, axis=1)
        new_vel = DECAY * vel + KICK * noise
        new_pos = jnp.clip(pos + STEP * (wind + new_vel), 0.0, upper[None, :, None])
        lz, tz = corner(new_pos[:, 2], LEV - 1)
        dest = target[:, 0][:, None]
        home = keys // MBC
        cell = keys % MBC
        grow = (dest // N_LON) * MBR + home // MBK
        gcol = (dest % N_LON) * MBK + home % MBK
        base = (grow * block_cols + gcol) * S
        indices = []
        values = []
        for s in range(S):
            for dl in range(2):
                weight = (1.0 - tz) if dl == 0 else tz
                indices.append(((base + s) * LEV + lz + dl) * MBC + cell)
                values.append((share[:, s] * weight).astype(jnp.bfloat16).astype(jnp.float32))
        total = total.at[jnp.stack(indices).reshape(-1)].add(jnp.stack(values).reshape(-1))
        return total, (new_pos, new_vel)

    items = (positions.reshape(devices, PB, 3, BLK), velocity.reshape(devices, PB, 3, BLK),
             increments.reshape(devices, PB, 3, BLK), mass.reshape(devices, PB, S, BLK),
             requests, block_slots.reshape(devices, PB), destinations.reshape(devices, PB, 1),
             cell_keys.reshape(devices, PB, BLK))
    conc, (new_pos, new_vel) = lax.scan(owner_step, conc, items)
    moved = new_pos.reshape(BLOCKS, 3, BLK)
    turbulence = new_vel.reshape(BLOCKS, 3, BLK)
    concentration = conc.reshape(MBR * N_LAT, block_cols, S, LEV, MBC)
    return moved, turbulence, concentration
```

```python
import jax
import jax.numpy as jnp
from jax import lax
from jax.experimental import pallas as pl
from jax.experimental.pallas import tpu as pltpu
from jax.sharding import PartitionSpec as P

BY = 8
BX = 16
MBC = 128
LEV = 40
S = 8
BLK = 128
MB = 16
Q = 2
CAP = 2
ROOM = Q * CAP

DECAY = 0.8
KICK = 0.6
STEP = 0.5

AXES = ("lat", "lon")
LOW16 = 0xFFFF
ROW_SCALE = 65535.0 / (BY - 1)
COL_SCALE = 65535.0 / (BX - 1)
LEV_SCALE = 65535.0 / (LEV - 1)
Z_ONE = float(1 << 21)
Z_MASK = (1 << 27) - 1
W_TOP = 6.1
W_SCALE = 65535.0 / (2 * W_TOP)
WZ_ONE = float(1 << 24)
M_SCALE = 32767.0
SAMPLE_UNROLL = 8
DEPOSIT_UNROLL = 4


def hat(offset):
    return jnp.maximum(0.0, 1.0 - jnp.abs(offset))


def fixed(value, scale, shift=0.0):
    return ((value + shift) * scale + 0.5).astype(jnp.int32)


def upper(word):
    return lax.shift_right_logical(word, jnp.int32(16)).astype(jnp.float32)


def lower(word):
    return (word & LOW16).astype(jnp.float32)


def whole(space=pltpu.VMEM):
    return pl.BlockSpec(memory_space=space)


def pack_kernel(
    slots, asked, targets, pos, mass, box, place1, place2, yx_rows, z_rows, seen1, seen2
):
    blocks, devices = pos.shape[0], box.shape[0]

    def clear(i, _):
        seen1[i] = 0
        seen2[i] = 0
        return 0

    lax.fori_loop(0, devices, clear, 0, unroll=8)
    box[:, 0:8, :] = jnp.full((devices, 8, BLK), -1, jnp.int32)
    yx_rows[...] = (fixed(pos[:, 0, :], ROW_SCALE) << 16) | fixed(pos[:, 1, :], COL_SCALE)
    z_rows[...] = (pos[:, 2, :] * Z_ONE).astype(jnp.int32)

    def put(b, _):
        slot = slots[b]
        tile = slot // Q
        rank = seen1[tile]
        seen1[tile] = rank + 1
        place1[b] = tile * ROOM + rank
        box[tile, pl.ds(2 * rank, 1), :] = yx_rows[pl.ds(b, 1), :]
        box[tile, pl.ds(2 * rank + 1, 1), :] = z_rows[pl.ds(b, 1), :] | (asked[slot] << 27)
        target = targets[b]
        turn = seen2[target]
        seen2[target] = turn + 1
        place2[b] = target * CAP + turn
        share = fixed(mass[b], M_SCALE)
        box[target, pl.ds(8 + 4 * turn, 4), :] = (share[0:4] << 16) | share[4:8]
        return 0

    lax.fori_loop(0, blocks, put, 0, unroll=4)


def sample_kernel(ids, count, box, winds, out, queue):
    devices = box.shape[0]

    def enlist(t, n):
        for r in range(ROOM):
            queue[n + r] = t * ROOM + r
        return n + count[t]

    n = lax.fori_loop(0, devices, enlist, 0, unroll=4)
    levels = lax.broadcasted_iota(jnp.int32, (LEV, BLK), 0).astype(jnp.float32)
    rows = lax.broadcasted_iota(jnp.int32, (BY, BLK), 0).astype(jnp.float32)
    cols = lax.broadcasted_iota(jnp.int32, (BX, BLK), 0).astype(jnp.float32)

    def step(i, _):
        for j in range(SAMPLE_UNROLL):
            item = queue[jnp.minimum(i * SAMPLE_UNROLL + j, n - 1)]
            src = item // ROOM
            rank = item % ROOM
            yx = box[src, pl.ds(2 * rank, 1), :]
            height = box[src, pl.ds(2 * rank + 1, 1), :]
            hy = hat(upper(yx) * (1.0 / ROW_SCALE) - rows)
            hx = hat(lower(yx) * (1.0 / COL_SCALE) - cols)
            z = (height & Z_MASK).astype(jnp.float32) * (1.0 / Z_ONE)
            wz = hat(z - levels).astype(jnp.bfloat16).astype(jnp.float32)
            flat = (hy[:, None, :] * hx[None, :, :]).reshape(MBC, BLK)
            high = flat.astype(jnp.bfloat16)
            low = (flat - high.astype(jnp.float32)).astype(jnp.bfloat16)
            met = winds[ids[item]]
            level_wind = jnp.dot(
                jnp.concatenate([met, met], axis=1),
                jnp.concatenate([high, low], axis=0),
                preferred_element_type=jnp.float32,
            )
            wind = [
                jnp.sum(level_wind[c * LEV : (c + 1) * LEV] * wz, axis=0, keepdims=True)
                for c in range(3)
            ]
            out[src, pl.ds(2 * rank, 1), :] = (fixed(wind[0], W_SCALE, W_TOP) << 16) | fixed(
                wind[1], W_SCALE, W_TOP
            )
            out[src, pl.ds(2 * rank + 1, 1), :] = (wind[2] * WZ_ONE).astype(jnp.int32)
        return 0

    lax.fori_loop(0, pl.cdiv(n, SAMPLE_UNROLL), step, 0)


def move_kernel(place1, place2, box, pos, vel, noise, keys, moved, turb, out, yx_rows, z_rows):
    blocks, devices = pos.shape[0], box.shape[0]

    def take(b, _):
        tile = place1[b] // ROOM
        rank = place1[b] % ROOM
        yx_rows[pl.ds(b, 1), :] = box[tile, pl.ds(2 * rank, 1), :]
        z_rows[pl.ds(b, 1), :] = box[tile, pl.ds(2 * rank + 1, 1), :]
        return 0

    lax.fori_loop(0, blocks, take, 0, unroll=8)
    yx = yx_rows[...]
    wind = (
        upper(yx) * (1.0 / W_SCALE) - W_TOP,
        lower(yx) * (1.0 / W_SCALE) - W_TOP,
        z_rows[...].astype(jnp.float32) * (1.0 / WZ_ONE),
    )
    for c, top in enumerate((BY - 1.0, BX - 1.0, LEV - 1.0)):
        fresh = DECAY * vel[:, c, :] + KICK * noise[:, c, :]
        turb[:, c, :] = fresh
        spot = jnp.clip(pos[:, c, :] + STEP * (wind[c] + fresh), 0.0, top)
        moved[:, c, :] = spot
    z_rows[...] = (keys[...] << 16) | fixed(spot, LEV_SCALE)
    out[...] = jnp.full(out.shape, -1, jnp.int32)

    def put(b, _):
        out[place2[b] // CAP, pl.ds(place2[b] % CAP, 1), :] = z_rows[pl.ds(b, 1), :]
        return 0

    lax.fori_loop(0, blocks, put, 0, unroll=8)


def deposit_kernel(homes, count, box, shares, total, queue):
    devices = box.shape[0]

    def enlist(t, n):
        for r in range(CAP):
            queue[n + r] = t * CAP + r
        return n + count[t]

    n = lax.fori_loop(0, devices, enlist, 0, unroll=4)
    total[...] = jnp.zeros(total.shape, jnp.float32)
    levels = lax.broadcasted_iota(jnp.int32, (LEV, BLK), 0).astype(jnp.float32)
    cells = lax.broadcasted_iota(jnp.int32, (MBC, BLK), 0)

    def step(i, _):
        for j in range(DEPOSIT_UNROLL):
            at = i * DEPOSIT_UNROLL + j
            item = queue[jnp.minimum(at, n - 1)]
            src = item // CAP
            rank = item % CAP
            word = box[src, pl.ds(rank, 1), :]
            packed = shares[src, pl.ds(8 + 4 * rank, 4), :]
            unit = jnp.where(at < n, 1.0 / M_SCALE, 0.0)
            share = jnp.concatenate([upper(packed), lower(packed)], axis=0) * unit
            vert = hat(lower(word) * (1.0 / LEV_SCALE) - levels)
            cell = (word >> 16) & (MBC - 1)
            weights = (share[:, None, :] * vert[None, :, :]).reshape(S * LEV, BLK)
            picks = jnp.where(cells == cell, 1.0, 0.0).astype(jnp.bfloat16)
            part = lax.dot_general(
                weights.astype(jnp.bfloat16),
                picks,
                (((1,), (1,)), ((), ())),
                preferred_element_type=jnp.float32,
            )
            home = homes[item]
            total[home] = total[home] + part
        return 0

    lax.fori_loop(0, pl.cdiv(n, DEPOSIT_UNROLL), step, 0)


def swap(box):
    return lax.all_to_all(box, AXES, split_axis=0, concat_axis=0, tiled=True)


def body(
    winds, positions, velocity, increments, mass, requests, block_slots, destinations, cell_keys
):
    devices = lax.axis_size("lat") * lax.axis_size("lon")
    blocks = positions.shape[0]
    params = pltpu.CompilerParams(vmem_limit_bytes=40 << 20)
    smem, vmem = whole(pltpu.SMEM), whole()
    i32, f32 = jnp.int32, jnp.float32
    box, place1, place2 = pl.pallas_call(
        pack_kernel,
        name="pack",
        out_shape=(
            jax.ShapeDtypeStruct((devices, 16, BLK), i32),
            jax.ShapeDtypeStruct((blocks,), i32),
            jax.ShapeDtypeStruct((blocks,), i32),
        ),
        in_specs=[smem, smem, smem, vmem, vmem],
        out_specs=(vmem, smem, smem),
        scratch_shapes=[
            pltpu.VMEM((blocks, BLK), i32),
            pltpu.VMEM((blocks, BLK), i32),
            pltpu.SMEM((devices,), i32),
            pltpu.SMEM((devices,), i32),
        ],
        compiler_params=params,
    )(block_slots.reshape(-1), requests.reshape(-1), destinations.reshape(-1), positions, mass)
    box = swap(box)
    ids = box[:, 1 : 2 * ROOM : 2, 0] >> 27
    local_wind = pl.pallas_call(
        sample_kernel,
        name="sample",
        out_shape=jax.ShapeDtypeStruct((devices, 8, BLK), i32),
        in_specs=[smem, smem, vmem, vmem],
        out_specs=vmem,
        scratch_shapes=[pltpu.SMEM((devices * ROOM + ROOM,), i32)],
        compiler_params=params,
    )(
        ids.reshape(-1),
        jnp.sum((ids >= 0).astype(i32), axis=1),
        box,
        winds.reshape(MB, 3 * LEV, MBC),
    )
    returned = swap(local_wind)
    moved, turbulence, outbox = pl.pallas_call(
        move_kernel,
        name="move",
        out_shape=(
            jax.ShapeDtypeStruct(positions.shape, f32),
            jax.ShapeDtypeStruct(positions.shape, f32),
            jax.ShapeDtypeStruct((devices, CAP, BLK), i32),
        ),
        in_specs=[smem, smem] + [vmem] * 5,
        out_specs=(vmem, vmem, vmem),
        scratch_shapes=[pltpu.VMEM((blocks, BLK), i32), pltpu.VMEM((blocks, BLK), i32)],
        compiler_params=params,
    )(place1, place2, returned, positions, velocity, increments, cell_keys)
    inbox = swap(outbox)
    homes = inbox[:, :, 0] >> 23
    total = pl.pallas_call(
        deposit_kernel,
        name="deposit",
        out_shape=jax.ShapeDtypeStruct((MB, S * LEV, MBC), f32),
        in_specs=[smem, smem, vmem, vmem],
        out_specs=vmem,
        scratch_shapes=[pltpu.SMEM((devices * CAP + CAP,), i32)],
        compiler_params=params,
    )(homes.reshape(-1), jnp.sum((homes >= 0).astype(i32), axis=1), inbox, box)
    return moved, turbulence, total.reshape(winds.shape[:2] + (S, LEV, MBC))


def solution(mesh):
    rows = P(AXES, None, None)
    pairs = P(AXES, None)
    tiles = P("lat", "lon", None, None, None)
    return jax.shard_map(
        body,
        mesh=mesh,
        in_specs=(tiles, rows, rows, rows, rows, rows, pairs, pairs, pairs),
        out_specs=(rows, rows, tiles),
        check_vma=False,
    )
```

```python
import jax
import jax.numpy as jnp
from jax import lax
from jax.experimental import pallas as pl
from jax.experimental.pallas import tpu as pltpu
from jax.sharding import PartitionSpec as P

BY = 8
BX = 16
MBC = 128
LEV = 40
S = 8
BLK = 128
MB = 16
Q = 2
CAP = 2
ROOM = Q * CAP

DECAY = 0.8
KICK = 0.6
STEP = 0.5

AXES = ("lat", "lon")
LOW16 = 0xFFFF
ROW_SCALE = 65535.0 / (BY - 1)
COL_SCALE = 65535.0 / (BX - 1)
LEV_SCALE = 65535.0 / (LEV - 1)
Z_ONE = float(1 << 22)
W_TOP = 6.1
W_SCALE = 65535.0 / (2 * W_TOP)
WZ_ONE = float(1 << 24)
M_SCALE = 32767.0
SAMPLE_UNROLL = 8
PAIR_UNROLL = 8

SHARE_ROW = 2 * ROOM
NOTE_ROW = SHARE_ROW + CAP * S // 2
ROWS = NOTE_ROW + 1
HOME_AT = ROOM
TAKEN_AT = HOME_AT + CAP
LANDED_AT = TAKEN_AT + 1


def hat(offset):
    return jnp.maximum(0.0, 1.0 - jnp.abs(offset))


def fixed(value, scale, shift=0.0):
    return ((value + shift) * scale + 0.5).astype(jnp.int32)


def upper(word):
    return lax.shift_right_logical(word, jnp.int32(16)).astype(jnp.float32)


def lower(word):
    return (word & LOW16).astype(jnp.float32)


def whole(space=pltpu.VMEM):
    return pl.BlockSpec(memory_space=space)


def read_notes(box, rows, notes, sem):
    devices = rows.shape[0]
    rows[...] = box[pl.ds(NOTE_ROW, devices, stride=ROWS), :]
    copy = pltpu.make_async_copy(rows, notes, sem)
    copy.start()
    copy.wait()


def pack_kernel(
    slots_hbm, asked_hbm, targets_hbm, keys_hbm, pos_hbm, mass_hbm,
    box, place1, place2,
    slots, asked, targets, keys, keys_head, pos, mass, spots, note_rows, notes, first, second, sems,
):
    blocks, devices = mass.shape[0], notes.shape[0]
    copies = [
        pltpu.make_async_copy(src, dst, sems.at[i])
        for i, (src, dst) in enumerate(
            (
                (slots_hbm, slots),
                (asked_hbm, asked),
                (targets_hbm, targets),
                (keys_hbm, keys),
                (pos_hbm, pos),
                (mass_hbm, mass),
            )
        )
    ]
    for copy in copies:
        copy.start()

    def clear(i, _):
        notes[i, TAKEN_AT] = 0
        notes[i, LANDED_AT] = 0
        return 0

    lax.fori_loop(0, devices, clear, 0, unroll=8)
    for copy in copies[:4]:
        copy.wait()

    def rank(b, _):
        slot = slots[0, b]
        tile = slot // Q
        turn = notes[tile, TAKEN_AT]
        notes[tile, TAKEN_AT] = turn + 1
        notes[tile, turn] = asked[slot % Q, tile]
        place1[b] = tile * ROOM + turn
        first[b] = tile * ROWS + 2 * turn
        target = targets[0, b]
        turn = notes[target, LANDED_AT]
        notes[target, LANDED_AT] = turn + 1
        notes[target, HOME_AT + turn] = keys[b, 0] // MBC
        place2[b] = target * CAP + turn
        second[b] = target * ROWS + SHARE_ROW + turn * (S // 2)
        return 0

    lax.fori_loop(0, blocks, rank, 0, unroll=4)
    noted = pltpu.make_async_copy(notes, note_rows, sems.at[len(copies)])
    noted.start()
    for copy in copies[4:]:
        copy.wait()
    spots[pl.ds(0, blocks, stride=2), :] = (fixed(pos[0], ROW_SCALE) << 16) | fixed(
        pos[1], COL_SCALE
    )
    spots[pl.ds(1, blocks, stride=2), :] = (pos[2] * Z_ONE).astype(jnp.int32)

    def put(b, _):
        box[pl.ds(first[b], 2), :] = spots[pl.ds(2 * b, 2), :]
        share = fixed(mass[b], M_SCALE)
        box[pl.ds(second[b], S // 2), :] = (share[0 : S // 2] << 16) | share[S // 2 :]
        return 0

    lax.fori_loop(0, blocks, put, 0, unroll=8)
    noted.wait()
    box[pl.ds(NOTE_ROW, devices, stride=ROWS), :] = note_rows[...]


def sample_kernel(box, winds, out, queue, rows_at, rows, notes, sem):
    devices = rows.shape[0]
    read_notes(box, rows, notes, sem)

    def enlist(t, n):
        for r in range(ROOM):
            queue[n + r] = t * ROOM + r
            rows_at[n + r] = notes[t, r]
        return n + notes[t, TAKEN_AT]

    n = lax.fori_loop(0, devices, enlist, 0, unroll=4)
    levels = lax.broadcasted_iota(jnp.int32, (LEV, BLK), 0).astype(jnp.float32)
    lats = lax.broadcasted_iota(jnp.int32, (BY, BLK), 0).astype(jnp.float32)
    lons = lax.broadcasted_iota(jnp.int32, (BX, BLK), 0).astype(jnp.float32)

    def step(i, _):
        for j in range(SAMPLE_UNROLL):
            at = jnp.minimum(i * SAMPLE_UNROLL + j, n - 1)
            item = queue[at]
            row = (item // ROOM) * ROWS + 2 * (item % ROOM)
            yx = box[pl.ds(row, 1), :]
            height = box[pl.ds(row + 1, 1), :]
            hy = hat(upper(yx) * (1.0 / ROW_SCALE) - lats)
            hx = hat(lower(yx) * (1.0 / COL_SCALE) - lons)
            wz = hat(height.astype(jnp.float32) * (1.0 / Z_ONE) - levels)
            wz = wz.astype(jnp.bfloat16).astype(jnp.float32)
            flat = (hy[:, None, :] * hx[None, :, :]).reshape(MBC, BLK)
            high = flat.astype(jnp.bfloat16)
            low = (flat - high.astype(jnp.float32)).astype(jnp.bfloat16)
            met = winds[rows_at[at]]
            level_wind = jnp.dot(
                jnp.concatenate([met, met], axis=1),
                jnp.concatenate([high, low], axis=0),
                preferred_element_type=jnp.float32,
            )
            wind = [
                jnp.sum(level_wind[c * LEV : (c + 1) * LEV] * wz, axis=0, keepdims=True)
                for c in range(3)
            ]
            out[pl.ds(2 * item, 1), :] = (fixed(wind[0], W_SCALE, W_TOP) << 16) | fixed(
                wind[1], W_SCALE, W_TOP
            )
            out[pl.ds(2 * item + 1, 1), :] = (wind[2] * WZ_ONE).astype(jnp.int32)
        return 0

    lax.fori_loop(0, pl.cdiv(n, SAMPLE_UNROLL), step, 0)


def order_kernel(box, items, homes, pairs, shares, rows, notes, starts, tally, sem):
    devices = rows.shape[0]
    read_notes(box, rows, notes, sem)

    def clear(i, _):
        items[i] = -1
        return 0

    lax.fori_loop(0, items.shape[0], clear, 0, unroll=4)

    def clear_home(i, _):
        homes[i] = 0
        return 0

    lax.fori_loop(0, homes.shape[0], clear_home, 0, unroll=2)
    for h in range(MB):
        tally[h] = 0

    def tell(t, _):
        landed = notes[t, LANDED_AT]
        for r in range(CAP):
            home = jnp.where(r < landed, notes[t, HOME_AT + r], MB)
            tally[home] = tally[home] + 1
        return 0

    tally[MB] = 0
    lax.fori_loop(0, devices, tell, 0, unroll=4)
    n = jnp.int32(0)
    for h in range(MB):
        starts[h] = n
        n = n + (tally[h] + 1) // 2 * 2
    starts[MB] = items.shape[0] - devices * CAP

    def place(t, _):
        landed = notes[t, LANDED_AT]
        for r in range(CAP):
            there = r < landed
            home = jnp.where(there, notes[t, HOME_AT + r], MB)
            at = starts[home]
            starts[home] = at + 1
            items[at] = jnp.where(there, t * CAP + r, -1)
            homes[at // 2] = jnp.where(there, home, 0)
        return 0

    lax.fori_loop(0, devices, place, 0, unroll=4)
    pairs[0] = n // 2

    def expand(i, _):
        for j in range(2 * PAIR_UNROLL):
            at = i * 2 * PAIR_UNROLL + j
            item = items[at]
            row = jnp.maximum(item, 0)
            packed = box[pl.ds((row // CAP) * ROWS + SHARE_ROW + (row % CAP) * (S // 2), S // 2), :]
            unit = jnp.where(item < 0, 0.0, 1.0 / M_SCALE)
            shares[at] = jnp.concatenate([upper(packed), lower(packed)], axis=0) * unit
        return 0

    lax.fori_loop(0, pl.cdiv(n, 2 * PAIR_UNROLL), expand, 0)


def move_kernel(place1, place2, pairs, box, pos, vel, noise, keys, moved, turb, out, winds, z_rows):
    blocks = z_rows.shape[0]

    def take(b, _):
        winds[pl.ds(2 * b, 2), :] = box[pl.ds(2 * place1[b], 2), :]
        return 0

    lax.fori_loop(0, blocks, take, 0, unroll=8)
    yx = winds[pl.ds(0, blocks, stride=2), :]
    wind = (
        upper(yx) * (1.0 / W_SCALE) - W_TOP,
        lower(yx) * (1.0 / W_SCALE) - W_TOP,
        winds[pl.ds(1, blocks, stride=2), :].astype(jnp.float32) * (1.0 / WZ_ONE),
    )
    for c, top in enumerate((BY - 1.0, BX - 1.0, LEV - 1.0)):
        fresh = DECAY * vel[c] + KICK * noise[c]
        turb[c] = fresh
        spot = jnp.clip(pos[c] + STEP * (wind[c] + fresh), 0.0, top)
        moved[c] = spot
    z_rows[...] = (keys[...] << 16) | fixed(spot, LEV_SCALE)

    def put(b, _):
        out[pl.ds(place2[b], 1), :] = z_rows[pl.ds(b, 1), :]
        return 0

    lax.fori_loop(0, blocks, put, 0, unroll=8)


def deposit_kernel(items, homes, pairs, box, shares, total):
    n = pairs[0]
    total[...] = jnp.zeros(total.shape, jnp.float32)
    levels = lax.broadcasted_iota(jnp.int32, (LEV, BLK), 0).astype(jnp.float32)
    cells = lax.broadcasted_iota(jnp.int32, (MBC, BLK), 0)

    def step(i, _):
        for j in range(PAIR_UNROLL):
            pair = i * PAIR_UNROLL + j
            weights, picks = [], []
            for half in range(2):
                at = 2 * pair + half
                word = box[pl.ds(jnp.maximum(items[at], 0), 1), :]
                vert = hat(lower(word) * (1.0 / LEV_SCALE) - levels)
                cell = (word >> 16) & (MBC - 1)
                share = shares[at]
                weights.append(
                    (share[:, None, :] * vert[None, :, :])
                    .reshape(S * LEV, BLK)
                    .astype(jnp.bfloat16)
                )
                picks.append(jnp.where(cells == cell, 1.0, 0.0).astype(jnp.bfloat16))
            part = lax.dot_general(
                jnp.concatenate(weights, axis=1),
                jnp.concatenate(picks, axis=1),
                (((1,), (1,)), ((), ())),
                preferred_element_type=jnp.float32,
            )
            home = homes[pair]
            total[home] = total[home] + part
        return 0

    lax.fori_loop(0, pl.cdiv(n, PAIR_UNROLL), step, 0)


def swap(box, devices):
    rows = box.shape[0] // devices
    if rows % 8 == 0:
        shape = (devices, rows, BLK)
    elif rows == 2:
        shape = (devices, rows, BLK)
    else:
        shape = (devices * rows, 1, BLK)
    box = lax.all_to_all(box.reshape(shape), AXES, split_axis=0, concat_axis=0, tiled=True)
    return box.reshape(devices * rows, BLK)


def body(
    winds, positions, velocity, increments, mass, requests, block_slots, destinations, cell_keys
):
    devices = lax.axis_size("lat") * lax.axis_size("lon")
    blocks = positions.shape[0]
    params = pltpu.CompilerParams(vmem_limit_bytes=40 << 20)
    smem, vmem, hbm = whole(pltpu.SMEM), whole(), whole(pltpu.HBM)
    i32, f32 = jnp.int32, jnp.float32
    dma = pltpu.SemaphoreType.DMA
    notes = [pltpu.VMEM((devices, BLK), i32), pltpu.SMEM((devices, BLK), i32)]
    by_part = (1, 0, 2)
    pos = positions.transpose(by_part)
    stay = lambda x: pltpu.with_memory_space_constraint(x, pltpu.HBM)
    box, place1, place2 = pl.pallas_call(
        pack_kernel,
        name="pack",
        out_shape=(
            jax.ShapeDtypeStruct((devices * ROWS, BLK), i32),
            jax.ShapeDtypeStruct((blocks,), i32),
            jax.ShapeDtypeStruct((blocks,), i32),
        ),
        in_specs=[hbm] * 6,
        out_specs=(vmem, smem, smem),
        scratch_shapes=[
            pltpu.SMEM((1, blocks), i32),
            pltpu.SMEM((Q, devices), i32),
            pltpu.SMEM((1, blocks), i32),
            pltpu.SMEM((blocks, BLK), i32),
            pltpu.SMEM((1, blocks), i32),
            pltpu.VMEM((3, blocks, BLK), f32),
            pltpu.VMEM((blocks, S, BLK), f32),
            pltpu.VMEM((2 * blocks, BLK), i32),
            *notes,
            pltpu.SMEM((blocks,), i32),
            pltpu.SMEM((blocks,), i32),
            dma((7,)),
        ],
        compiler_params=params,
    )(
        stay(block_slots.transpose(1, 0)),
        stay(requests.reshape(devices, Q).transpose(1, 0)),
        stay(destinations.transpose(1, 0)),
        stay(cell_keys),
        stay(pos),
        stay(mass),
    )
    box = swap(box, devices)
    local_wind = pl.pallas_call(
        sample_kernel,
        name="sample",
        out_shape=jax.ShapeDtypeStruct((devices * 2 * ROOM, BLK), i32),
        in_specs=[vmem, vmem],
        out_specs=vmem,
        scratch_shapes=[
            pltpu.SMEM((devices * ROOM + ROOM,), i32),
            pltpu.SMEM((devices * ROOM + ROOM,), i32),
            *notes,
            dma,
        ],
        compiler_params=params,
    )(box, winds.reshape(MB, 3 * LEV, MBC))
    room = devices * CAP + MB + 2 * PAIR_UNROLL
    items, homes, pairs, shares = pl.pallas_call(
        order_kernel,
        name="order",
        cost_estimate=pl.CostEstimate(flops=10**9, bytes_accessed=20 << 20, transcendentals=0),
        out_shape=(
            jax.ShapeDtypeStruct((room + devices * CAP,), i32),
            jax.ShapeDtypeStruct(((room + devices * CAP) // 2 + 1,), i32),
            jax.ShapeDtypeStruct((8,), i32),
            jax.ShapeDtypeStruct((room, S, BLK), f32),
        ),
        in_specs=[vmem],
        out_specs=(smem, smem, smem, vmem),
        scratch_shapes=[
            *notes,
            pltpu.SMEM((MB + 1,), i32),
            pltpu.SMEM((MB + 1,), i32),
            dma,
        ],
        compiler_params=params,
    )(box)
    returned = swap(local_wind, devices)
    moved, turbulence, outbox = pl.pallas_call(
        move_kernel,
        name="move",
        out_shape=(
            jax.ShapeDtypeStruct(pos.shape, f32),
            jax.ShapeDtypeStruct(pos.shape, f32),
            jax.ShapeDtypeStruct((devices * CAP, BLK), i32),
        ),
        in_specs=[smem, smem, smem] + [vmem] * 5,
        out_specs=(vmem, vmem, vmem),
        scratch_shapes=[pltpu.VMEM((2 * blocks, BLK), i32), pltpu.VMEM((blocks, BLK), i32)],
        compiler_params=params,
    )(
        place1,
        place2,
        pairs,
        returned,
        pos,
        velocity.transpose(by_part),
        increments.transpose(by_part),
        cell_keys,
    )
    inbox = swap(outbox, devices)
    total = pl.pallas_call(
        deposit_kernel,
        name="deposit",
        out_shape=jax.ShapeDtypeStruct((MB, S * LEV, MBC), f32),
        in_specs=[smem, smem, smem, vmem, vmem],
        out_specs=vmem,
        compiler_params=params,
    )(items, homes, pairs, inbox, shares)
    return (
        moved.transpose(by_part),
        turbulence.transpose(by_part),
        total.reshape(winds.shape[:2] + (S, LEV, MBC)),
    )


def solution(mesh):
    rows = P(AXES, None, None)
    pairs = P(AXES, None)
    tiles = P("lat", "lon", None, None, None)
    return jax.shard_map(
        body,
        mesh=mesh,
        in_specs=(tiles, rows, rows, rows, rows, rows, pairs, pairs, pairs),
        out_specs=(rows, rows, tiles),
        check_vma=False,
    )
```

```python
import jax
import jax.numpy as jnp
from jax import lax
from jax.experimental import pallas as pl
from jax.experimental.pallas import tpu as pltpu
from jax.sharding import PartitionSpec as P

BY = 8
BX = 16
MBC = 128
LEV = 40
S = 8
BLK = 128
MB = 16
Q = 2
CAP = 2
ROOM = Q * CAP

DECAY = 0.8
KICK = 0.6
STEP = 0.5

AXES = ("lat", "lon")
LOW16 = 0xFFFF
ROW_SCALE = 65535.0 / (BY - 1)
COL_SCALE = 65535.0 / (BX - 1)
LEV_SCALE = 65535.0 / (LEV - 1)
Z_ONE = float(1 << 22)
W_TOP = 6.1
W_SCALE = 65535.0 / (2 * W_TOP)
M_SCALE = 32767.0
SAMPLE_UNROLL = 12
PAIR_UNROLL = 16

SHARE_ROW = 2 * ROOM
NOTE_ROW = SHARE_ROW + CAP * S // 2
ROWS = NOTE_ROW + 1
WIND_ROWS = ROOM + ROOM // 2
HOME_AT = ROOM
TAKEN_AT = HOME_AT + CAP
LANDED_AT = TAKEN_AT + 1


def hat(offset):
    return jnp.maximum(0.0, 1.0 - jnp.abs(offset))


def fixed(value, scale, shift=0.0):
    return ((value + shift) * scale + 0.5).astype(jnp.int32)


def upper(word):
    return lax.shift_right_logical(word, jnp.int32(16)).astype(jnp.float32)


def lower(word):
    return (word & LOW16).astype(jnp.float32)


def whole(space=pltpu.VMEM):
    return pl.BlockSpec(memory_space=space)


def read_notes(box, rows, notes, sem):
    devices = rows.shape[0]
    rows[...] = box[pl.ds(NOTE_ROW, devices, stride=ROWS), :]
    copy = pltpu.make_async_copy(rows, notes, sem)
    copy.start()
    copy.wait()


def pack_kernel(
    slots_hbm, asked_hbm, targets_hbm, keys_hbm, pos_hbm, mass_hbm,
    box, places,
    slots, asked, targets, keys, pos, mass, spots, ranks, sems,
):
    blocks, devices = mass.shape[0], asked.shape[1]
    copies = [
        pltpu.make_async_copy(src, dst, sems.at[i])
        for i, (src, dst) in enumerate(
            (
                (slots_hbm, slots),
                (targets_hbm, targets),
                (asked_hbm, asked),
                (keys_hbm, keys),
                (pos_hbm, pos),
                (mass_hbm, mass),
            )
        )
    ]
    for copy in copies:
        copy.start()
    square = (blocks, blocks)
    down = lax.broadcasted_iota(jnp.int32, square, 0)
    along = lax.broadcasted_iota(jnp.int32, square, 1)

    def stand(row):
        return jnp.broadcast_to(row.astype(jnp.float32), square).T.astype(jnp.int32)

    def rank(row):
        same = (stand(row) == row) & (down < along)
        return jnp.sum(jnp.where(same, 1.0, 0.0), axis=0, keepdims=True).astype(jnp.int32)

    copies[0].wait()
    slot = slots[...]
    tile = slot // Q
    order = rank(tile)
    copies[1].wait()
    target = targets[...]
    turn = rank(target)
    ranks[0:1, :] = tile * ROWS + 2 * order
    ranks[1:2, :] = target * ROWS + SHARE_ROW + turn * (S // 2)
    ranks[2:3, :] = tile * WIND_ROWS + order
    ranks[3:4, :] = tile * WIND_ROWS + ROOM + order // 2
    ranks[4:5, :] = 16 - 16 * (order % 2)
    ranks[5:6, :] = target * CAP + turn
    ranked = pltpu.make_async_copy(ranks, places, sems.at[len(copies)])
    ranked.start()
    slot_down = stand(slot)
    tile_down = slot_down // Q
    copies[2].wait()
    met = jnp.where(slot_down % Q == 0, asked[0:1, :], asked[1:2, :])
    met = jnp.where(tile_down == along, met, 0).astype(jnp.float32)
    met = jnp.sum(met, axis=1, keepdims=True)
    copies[3].wait()
    home = (keys[:, 0:1] // MBC).astype(jnp.float32)
    said = jnp.where(along == stand(order), met, 0.0) + jnp.where(along == TAKEN_AT, 1.0, 0.0)
    more = jnp.where(along == HOME_AT + stand(turn), home, 0.0) + jnp.where(
        along == LANDED_AT, 1.0, 0.0
    )
    mine = jnp.concatenate([down == tile, down == target], axis=1)
    notes = jnp.dot(
        jnp.where(mine, 1.0, 0.0).astype(jnp.bfloat16),
        jnp.concatenate([said, more], axis=0).astype(jnp.bfloat16),
        preferred_element_type=jnp.float32,
    )
    box[pl.ds(NOTE_ROW, devices, stride=ROWS), :] = notes.astype(jnp.int32)
    copies[4].wait()
    spots[pl.ds(0, blocks, stride=2), :] = (fixed(pos[0], ROW_SCALE) << 16) | fixed(
        pos[1], COL_SCALE
    )
    spots[pl.ds(1, blocks, stride=2), :] = (pos[2] * Z_ONE).astype(jnp.int32)
    copies[5].wait()
    ranked.wait()

    def put(b, _):
        box[pl.ds(places[0, b], 2), :] = spots[pl.ds(2 * b, 2), :]
        share = fixed(mass[b], M_SCALE)
        box[pl.ds(places[1, b], S // 2), :] = (share[0 : S // 2] << 16) | share[S // 2 :]
        return 0

    lax.fori_loop(0, blocks, put, 0, unroll=8)


def sample_kernel(box, winds, out, queue, found, rows, notes, sem):
    devices = rows.shape[0]
    read_notes(box, rows, notes, sem)

    def enlist(t, n):
        for r in range(ROOM):
            queue[n + r] = t * ROOM + r
        return n + notes[t, TAKEN_AT]

    n = lax.fori_loop(0, devices, enlist, 0, unroll=4)
    levels = lax.broadcasted_iota(jnp.int32, (LEV, BLK), 0).astype(jnp.float32)
    lats = lax.broadcasted_iota(jnp.int32, (BY, BLK), 0).astype(jnp.float32)
    lons = lax.broadcasted_iota(jnp.int32, (BX, BLK), 0).astype(jnp.float32)

    def step(i, _):
        for j in range(SAMPLE_UNROLL):
            item = queue[jnp.minimum(i * SAMPLE_UNROLL + j, n - 1)]
            row = (item // ROOM) * ROWS + 2 * (item % ROOM)
            yx = box[pl.ds(row, 1), :]
            height = box[pl.ds(row + 1, 1), :]
            hy = hat(upper(yx) * (1.0 / ROW_SCALE) - lats)
            hx = hat(lower(yx) * (1.0 / COL_SCALE) - lons)
            wz = hat(height.astype(jnp.float32) * (1.0 / Z_ONE) - levels)
            wz = wz.astype(jnp.bfloat16).astype(jnp.float32)
            flat = (hy[:, None, :] * hx[None, :, :]).reshape(MBC, BLK)
            high = flat.astype(jnp.bfloat16)
            low = (flat - high.astype(jnp.float32)).astype(jnp.bfloat16)
            met = winds[notes[item // ROOM, item % ROOM]]
            level_wind = jnp.dot(
                jnp.concatenate([met, met], axis=1),
                jnp.concatenate([high, low], axis=0),
                preferred_element_type=jnp.float32,
            )
            wind = [
                jnp.sum(level_wind[c * LEV : (c + 1) * LEV] * wz, axis=0, keepdims=True)
                for c in range(3)
            ]
            found[pl.ds(2 * item, 1), :] = (fixed(wind[0], W_SCALE, W_TOP) << 16) | fixed(
                wind[1], W_SCALE, W_TOP
            )
            found[pl.ds(2 * item + 1, 1), :] = fixed(wind[2], W_SCALE, W_TOP)
        return 0

    lax.fori_loop(0, pl.cdiv(n, SAMPLE_UNROLL), step, 0)

    def every(r):
        return found[pl.ds(r, devices, stride=2 * ROOM), :]

    for r in range(ROOM):
        out[pl.ds(r, devices, stride=WIND_ROWS), :] = every(2 * r)
    for r in range(0, ROOM, 2):
        out[pl.ds(ROOM + r // 2, devices, stride=WIND_ROWS), :] = (every(2 * r + 1) << 16) | (
            every(2 * r + 3) & LOW16
        )


def order_kernel(box, items, homes, pairs, shares, rows, notes, starts, tally, sem):
    devices = rows.shape[0]
    read_notes(box, rows, notes, sem)

    def clear(i, _):
        items[i] = -1
        return 0

    lax.fori_loop(0, items.shape[0], clear, 0, unroll=4)

    def clear_home(i, _):
        homes[i] = 0
        return 0

    lax.fori_loop(0, homes.shape[0], clear_home, 0, unroll=2)
    for h in range(MB):
        tally[h] = 0

    def tell(t, _):
        landed = notes[t, LANDED_AT]
        for r in range(CAP):
            home = jnp.where(r < landed, notes[t, HOME_AT + r], MB)
            tally[home] = tally[home] + 1
        return 0

    tally[MB] = 0
    lax.fori_loop(0, devices, tell, 0, unroll=4)
    n = jnp.int32(0)
    for h in range(MB):
        starts[h] = n
        n = n + (tally[h] + 1) // 2 * 2
    starts[MB] = items.shape[0] - devices * CAP

    def place(t, _):
        landed = notes[t, LANDED_AT]
        for r in range(CAP):
            there = r < landed
            home = jnp.where(there, notes[t, HOME_AT + r], MB)
            at = starts[home]
            starts[home] = at + 1
            items[at] = jnp.where(there, t * CAP + r, -1)
            homes[at // 2] = jnp.where(there, home, 0)
        return 0

    lax.fori_loop(0, devices, place, 0, unroll=4)
    pairs[0] = n // 2

    def expand(i, _):
        for j in range(2 * PAIR_UNROLL):
            at = i * 2 * PAIR_UNROLL + j
            item = items[at]
            row = jnp.maximum(item, 0)
            packed = box[pl.ds((row // CAP) * ROWS + SHARE_ROW + (row % CAP) * (S // 2), S // 2), :]
            unit = jnp.where(item < 0, 0.0, 1.0 / M_SCALE)
            shares[pl.ds(S * at, S), :] = (
                jnp.concatenate([upper(packed), lower(packed)], axis=0) * unit
            )
        return 0

    lax.fori_loop(0, pl.cdiv(n, 2 * PAIR_UNROLL), expand, 0)


def move_kernel(places, pairs, box, pos, vel, noise, keys, moved, turb, out, yx_rows, z_rows):
    blocks = z_rows.shape[0]

    def take(b, _):
        yx_rows[pl.ds(b, 1), :] = box[pl.ds(places[2, b], 1), :]
        z_rows[pl.ds(b, 1), :] = lax.shift_right_logical(
            box[pl.ds(places[3, b], 1), :], jnp.full((1, BLK), places[4, b], jnp.int32)
        )
        return 0

    lax.fori_loop(0, blocks, take, 0, unroll=8)
    yx = yx_rows[...]
    wind = [part * (1.0 / W_SCALE) - W_TOP for part in (upper(yx), lower(yx), lower(z_rows[...]))]
    for c, top in enumerate((BY - 1.0, BX - 1.0, LEV - 1.0)):
        fresh = DECAY * vel[c] + KICK * noise[c]
        turb[c] = fresh
        spot = jnp.clip(pos[c] + STEP * (wind[c] + fresh), 0.0, top)
        moved[c] = spot
    z_rows[...] = (keys[...] << 16) | fixed(spot, LEV_SCALE)

    def put(b, _):
        out[pl.ds(places[5, b], 1), :] = z_rows[pl.ds(b, 1), :]
        return 0

    lax.fori_loop(0, blocks, put, 0, unroll=8)


def deposit_kernel(items, homes, pairs, box, shares, total):
    n = pairs[0]
    total[...] = jnp.zeros(total.shape, jnp.float32)
    level = lax.broadcasted_iota(jnp.int32, (8, BLK), 0).astype(jnp.float32)
    cells = lax.broadcasted_iota(jnp.int32, (MBC, BLK), 0).astype(jnp.float32)
    cells = cells.astype(jnp.bfloat16)
    one, none = jnp.bfloat16(1), jnp.bfloat16(0)

    def step(i, _):
        for j in range(PAIR_UNROLL):
            pair = i * PAIR_UNROLL + j
            weights, picks = [], []
            for half in range(2):
                at = 2 * pair + half
                row = jnp.maximum(items[at], 0)
                word = box[pl.ds(row, 1), :]
                height = jnp.broadcast_to(lower(word) * (1.0 / LEV_SCALE), (8, BLK))
                vert = [hat(height - (level + 8.0 * k)) for k in range(LEV // 8)]
                held = [
                    shares[pl.ds(S * at + s, 8, stride=0), :] * part for s in range(S) for part in vert
                ]
                weights.append(jnp.concatenate(held, axis=0).astype(jnp.bfloat16))
                cell = (word >> 16) & (MBC - 1)
                cell = cell.astype(jnp.float32).astype(jnp.bfloat16)
                picks.append(jnp.where(cells == cell, one, none))
            part = lax.dot_general(
                jnp.concatenate(weights, axis=1),
                jnp.concatenate(picks, axis=1),
                (((1,), (1,)), ((), ())),
                preferred_element_type=jnp.float32,
            )
            home = homes[pair]
            total[home] = total[home] + part
        return 0

    lax.fori_loop(0, pl.cdiv(n, PAIR_UNROLL), step, 0)


def swap(box, devices):
    rows = box.shape[0] // devices
    step = 8 if rows % 8 == 0 else 2 if rows % 2 == 0 else 1
    whole_box = box.reshape(devices * rows // step, step, BLK)
    arrived = lax.all_to_all(whole_box, AXES, split_axis=0, concat_axis=0, tiled=True)
    return arrived.reshape(box.shape)


def body(
    winds, positions, velocity, increments, mass, requests, block_slots, destinations, cell_keys
):
    devices = lax.axis_size("lat") * lax.axis_size("lon")
    blocks = positions.shape[0]
    params = pltpu.CompilerParams(vmem_limit_bytes=40 << 20)
    smem, vmem, hbm = whole(pltpu.SMEM), whole(), whole(pltpu.HBM)
    i32, f32 = jnp.int32, jnp.float32
    dma = pltpu.SemaphoreType.DMA
    notes = [pltpu.VMEM((devices, BLK), i32), pltpu.SMEM((devices, BLK), i32)]
    by_part = (1, 0, 2)
    pos = positions.transpose(by_part)
    stay = lambda x: pltpu.with_memory_space_constraint(x, pltpu.HBM)
    box, places = pl.pallas_call(
        pack_kernel,
        name="pack",
        out_shape=(
            jax.ShapeDtypeStruct((devices * ROWS, BLK), i32),
            jax.ShapeDtypeStruct((8, blocks), i32),
        ),
        in_specs=[hbm] * 6,
        out_specs=(vmem, smem),
        scratch_shapes=[
            pltpu.VMEM((1, blocks), i32),
            pltpu.VMEM((Q, devices), i32),
            pltpu.VMEM((1, blocks), i32),
            pltpu.VMEM((blocks, BLK), i32),
            pltpu.VMEM((3, blocks, BLK), f32),
            pltpu.VMEM((blocks, S, BLK), f32),
            pltpu.VMEM((2 * blocks, BLK), i32),
            pltpu.VMEM((8, blocks), i32),
            dma((7,)),
        ],
        compiler_params=params,
    )(
        stay(block_slots.transpose(1, 0)),
        stay(requests.reshape(devices, Q).transpose(1, 0)),
        stay(destinations.transpose(1, 0)),
        stay(cell_keys),
        stay(pos),
        stay(mass),
    )
    box = swap(box, devices)
    local_wind = pl.pallas_call(
        sample_kernel,
        name="sample",
        out_shape=jax.ShapeDtypeStruct((devices * WIND_ROWS, BLK), i32),
        in_specs=[vmem, vmem],
        out_specs=vmem,
        scratch_shapes=[
            pltpu.SMEM((devices * ROOM + ROOM,), i32),
            pltpu.VMEM((devices * 2 * ROOM, BLK), i32),
            *notes,
            dma,
        ],
        compiler_params=params,
    )(box, winds.reshape(MB, 3 * LEV, MBC))
    room = devices * CAP + MB + 2 * PAIR_UNROLL
    items, homes, pairs, shares = pl.pallas_call(
        order_kernel,
        name="order",
        cost_estimate=pl.CostEstimate(flops=10**9, bytes_accessed=20 << 20, transcendentals=0),
        out_shape=(
            jax.ShapeDtypeStruct((room + devices * CAP,), i32),
            jax.ShapeDtypeStruct(((room + devices * CAP) // 2 + 1,), i32),
            jax.ShapeDtypeStruct((8,), i32),
            jax.ShapeDtypeStruct((room * S, BLK), f32),
        ),
        in_specs=[vmem],
        out_specs=(smem, smem, smem, vmem),
        scratch_shapes=[
            *notes,
            pltpu.SMEM((MB + 1,), i32),
            pltpu.SMEM((MB + 1,), i32),
            dma,
        ],
        compiler_params=params,
    )(box)
    returned = swap(local_wind, devices)
    moved, turbulence, outbox = pl.pallas_call(
        move_kernel,
        name="move",
        out_shape=(
            jax.ShapeDtypeStruct(pos.shape, f32),
            jax.ShapeDtypeStruct(pos.shape, f32),
            jax.ShapeDtypeStruct((devices * CAP, BLK), i32),
        ),
        in_specs=[smem, smem] + [vmem] * 5,
        out_specs=(vmem, vmem, vmem),
        scratch_shapes=[pltpu.VMEM((blocks, BLK), i32), pltpu.VMEM((blocks, BLK), i32)],
        compiler_params=params,
    )(
        places,
        pairs,
        returned,
        pos,
        velocity.transpose(by_part),
        increments.transpose(by_part),
        cell_keys,
    )
    inbox = swap(outbox, devices)
    total = pl.pallas_call(
        deposit_kernel,
        name="deposit",
        out_shape=jax.ShapeDtypeStruct((MB, S * LEV, MBC), f32),
        in_specs=[smem, smem, smem, vmem, vmem],
        out_specs=vmem,
        compiler_params=params,
    )(items, homes, pairs, inbox, shares)
    return (
        moved.transpose(by_part),
        turbulence.transpose(by_part),
        total.reshape(winds.shape[:2] + (S, LEV, MBC)),
    )


def solution(mesh):
    rows = P(AXES, None, None)
    pairs = P(AXES, None)
    tiles = P("lat", "lon", None, None, None)
    return jax.shard_map(
        body,
        mesh=mesh,
        in_specs=(tiles, rows, rows, rows, rows, rows, pairs, pairs, pairs),
        out_specs=(rows, rows, tiles),
        check_vma=False,
    )
```

```python
import jax
import jax.numpy as jnp
from jax import lax
from jax.experimental import pallas as pl
from jax.experimental.pallas import tpu as pltpu
from jax.sharding import PartitionSpec as P

BY = 8
BX = 16
MBC = 128
LEV = 40
S = 8
BLK = 128
MB = 16
Q = 2
CAP = 2
ROOM = Q * CAP

DECAY = 0.8
KICK = 0.6
STEP = 0.5

AXES = ("lat", "lon")
LOW16 = 0xFFFF
ROW_SCALE = 65535.0 / (BY - 1)
COL_SCALE = 65535.0 / (BX - 1)
LEV_SCALE = 65535.0 / (LEV - 1)
Z_ONE = float(1 << 22)
W_TOP = 6.1
W_SCALE = 65535.0 / (2 * W_TOP)
M_SCALE = 32767.0
SAMPLE_UNROLL = 12
PAIR_UNROLL = 16

SHARE_ROW = 2 * ROOM
NOTE_ROW = SHARE_ROW + CAP * S // 2
ROWS = NOTE_ROW + 1
WIND_ROWS = ROOM + ROOM // 2
HOME_AT = ROOM
TAKEN_AT = HOME_AT + CAP
LANDED_AT = TAKEN_AT + 1


def hat(offset):
    return jnp.maximum(0.0, 1.0 - jnp.abs(offset))


def fixed(value, scale, shift=0.0):
    return ((value + shift) * scale + 0.5).astype(jnp.int32)


def upper(word):
    return lax.shift_right_logical(word, jnp.int32(16)).astype(jnp.float32)


def lower(word):
    return (word & LOW16).astype(jnp.float32)


def whole(space=pltpu.VMEM):
    return pl.BlockSpec(memory_space=space)


def read_notes(box, rows, notes, sem):
    devices = notes.shape[1]
    sent = box[pl.ds(NOTE_ROW, devices, stride=ROWS), :].astype(jnp.float32)
    rows[...] = sent.T[0 : notes.shape[0], :].astype(jnp.int32)
    copy = pltpu.make_async_copy(rows, notes, sem)
    copy.start()
    copy.wait()


def pack_kernel(
    slots_hbm, asked_hbm, targets_hbm, keys_hbm, pos_hbm, mass_hbm,
    box, places,
    slots, asked, targets, keys, pos, mass, spots, ranks, sems,
):
    blocks, devices = mass.shape[0], asked.shape[1]
    copies = [
        pltpu.make_async_copy(src, dst, sems.at[i])
        for i, (src, dst) in enumerate(
            (
                (slots_hbm, slots),
                (targets_hbm, targets),
                (asked_hbm, asked),
                (keys_hbm, keys),
                (pos_hbm, pos),
                (mass_hbm, mass),
            )
        )
    ]
    for copy in copies:
        copy.start()
    square = (blocks, blocks)
    down = lax.broadcasted_iota(jnp.int32, square, 0)
    along = lax.broadcasted_iota(jnp.int32, square, 1)

    def stand(row):
        return jnp.broadcast_to(row.astype(jnp.float32), square).T.astype(jnp.int32)

    def rank(row):
        same = (stand(row) == row) & (down < along)
        return jnp.sum(jnp.where(same, 1.0, 0.0), axis=0, keepdims=True).astype(jnp.int32)

    copies[0].wait()
    slot = slots[...]
    tile = slot // Q
    order = rank(tile)
    copies[1].wait()
    target = targets[...]
    turn = rank(target)
    ranks[0:1, :] = tile * ROWS + 2 * order
    ranks[1:2, :] = target * ROWS + SHARE_ROW + turn * (S // 2)
    ranks[2:3, :] = tile * WIND_ROWS + order
    ranks[3:4, :] = tile * WIND_ROWS + ROOM + order // 2
    ranks[4:5, :] = 16 - 16 * (order % 2)
    ranks[5:6, :] = target * CAP + turn
    ranked = pltpu.make_async_copy(ranks, places, sems.at[len(copies)])
    ranked.start()
    slot_down = stand(slot)
    tile_down = slot_down // Q
    copies[2].wait()
    met = jnp.where(slot_down % Q == 0, asked[0:1, :], asked[1:2, :])
    met = jnp.where(tile_down == along, met, 0).astype(jnp.float32)
    met = jnp.sum(met, axis=1, keepdims=True)
    copies[3].wait()
    home = (keys[:, 0:1] // MBC).astype(jnp.float32)
    said = jnp.where(along == stand(order), met, 0.0) + jnp.where(along == TAKEN_AT, 1.0, 0.0)
    more = jnp.where(along == HOME_AT + stand(turn), home, 0.0) + jnp.where(
        along == LANDED_AT, 1.0, 0.0
    )
    mine = jnp.concatenate([down == tile, down == target], axis=1)
    notes = jnp.dot(
        jnp.where(mine, 1.0, 0.0).astype(jnp.bfloat16),
        jnp.concatenate([said, more], axis=0).astype(jnp.bfloat16),
        preferred_element_type=jnp.float32,
    )
    box[pl.ds(NOTE_ROW, devices, stride=ROWS), :] = notes.astype(jnp.int32)
    copies[4].wait()
    spots[pl.ds(0, blocks, stride=2), :] = (fixed(pos[0], ROW_SCALE) << 16) | fixed(
        pos[1], COL_SCALE
    )
    spots[pl.ds(1, blocks, stride=2), :] = (pos[2] * Z_ONE).astype(jnp.int32)
    copies[5].wait()
    ranked.wait()

    def put(b, _):
        box[pl.ds(places[0, b], 2), :] = spots[pl.ds(2 * b, 2), :]
        share = fixed(mass[b], M_SCALE)
        box[pl.ds(places[1, b], S // 2), :] = (share[0 : S // 2] << 16) | share[S // 2 :]
        return 0

    lax.fori_loop(0, blocks, put, 0, unroll=8)


def sample_kernel(box, winds, out, queue, found, rows, notes, sem):
    devices = notes.shape[1]
    read_notes(box, rows, notes, sem)

    def enlist(t, n):
        for r in range(ROOM):
            queue[n + r] = t * ROOM + r
        return n + notes[TAKEN_AT, t]

    n = lax.fori_loop(0, devices, enlist, 0, unroll=4)
    levels = lax.broadcasted_iota(jnp.int32, (LEV, BLK), 0).astype(jnp.float32)
    lats = lax.broadcasted_iota(jnp.int32, (BY, BLK), 0).astype(jnp.float32)
    lons = lax.broadcasted_iota(jnp.int32, (BX, BLK), 0).astype(jnp.float32)

    def step(i, _):
        for j in range(SAMPLE_UNROLL):
            item = queue[jnp.minimum(i * SAMPLE_UNROLL + j, n - 1)]
            row = (item // ROOM) * ROWS + 2 * (item % ROOM)
            yx = box[pl.ds(row, 1), :]
            height = box[pl.ds(row + 1, 1), :]
            hy = hat(upper(yx) * (1.0 / ROW_SCALE) - lats)
            hx = hat(lower(yx) * (1.0 / COL_SCALE) - lons)
            wz = hat(height.astype(jnp.float32) * (1.0 / Z_ONE) - levels)
            wz = wz.astype(jnp.bfloat16).astype(jnp.float32)
            flat = (hy[:, None, :] * hx[None, :, :]).reshape(MBC, BLK)
            high = flat.astype(jnp.bfloat16)
            low = (flat - high.astype(jnp.float32)).astype(jnp.bfloat16)
            met = winds[notes[item % ROOM, item // ROOM]]
            level_wind = jnp.dot(met, high, preferred_element_type=jnp.float32) + jnp.dot(
                met, low, preferred_element_type=jnp.float32
            )
            wind = [
                jnp.sum(level_wind[c * LEV : (c + 1) * LEV] * wz, axis=0, keepdims=True)
                for c in range(3)
            ]
            found[pl.ds(2 * item, 1), :] = (fixed(wind[0], W_SCALE, W_TOP) << 16) | fixed(
                wind[1], W_SCALE, W_TOP
            )
            found[pl.ds(2 * item + 1, 1), :] = fixed(wind[2], W_SCALE, W_TOP)
        return 0

    lax.fori_loop(0, pl.cdiv(n, SAMPLE_UNROLL), step, 0)

    def every(r):
        return found[pl.ds(r, devices, stride=2 * ROOM), :]

    for r in range(ROOM):
        out[pl.ds(r, devices, stride=WIND_ROWS), :] = every(2 * r)
    for r in range(0, ROOM, 2):
        out[pl.ds(ROOM + r // 2, devices, stride=WIND_ROWS), :] = (every(2 * r + 1) << 16) | (
            every(2 * r + 3) & LOW16
        )


def order_kernel(box, items, homes, pairs, shares, rows, notes, starts, tally, sem):
    devices = notes.shape[1]
    read_notes(box, rows, notes, sem)

    def clear(i, _):
        items[i] = -1
        return 0

    lax.fori_loop(0, items.shape[0], clear, 0, unroll=4)

    def clear_home(i, _):
        homes[i] = 0
        return 0

    lax.fori_loop(0, homes.shape[0], clear_home, 0, unroll=2)
    for h in range(MB):
        tally[h] = 0

    def tell(t, _):
        landed = notes[LANDED_AT, t]
        for r in range(CAP):
            home = jnp.where(r < landed, notes[HOME_AT + r, t], MB)
            tally[home] = tally[home] + 1
        return 0

    tally[MB] = 0
    lax.fori_loop(0, devices, tell, 0, unroll=4)
    n = jnp.int32(0)
    for h in range(MB):
        starts[h] = n
        n = n + (tally[h] + 1) // 2 * 2
    starts[MB] = items.shape[0] - devices * CAP

    def place(t, _):
        landed = notes[LANDED_AT, t]
        for r in range(CAP):
            there = r < landed
            home = jnp.where(there, notes[HOME_AT + r, t], MB)
            at = starts[home]
            starts[home] = at + 1
            items[at] = jnp.where(there, t * CAP + r, -1)
            homes[at // 2] = jnp.where(there, home, 0)
        return 0

    lax.fori_loop(0, devices, place, 0, unroll=4)
    pairs[0] = n // 2

    def expand(i, _):
        for j in range(2 * PAIR_UNROLL):
            at = i * 2 * PAIR_UNROLL + j
            item = items[at]
            row = jnp.maximum(item, 0)
            packed = box[pl.ds((row // CAP) * ROWS + SHARE_ROW + (row % CAP) * (S // 2), S // 2), :]
            unit = jnp.where(item < 0, 0.0, 1.0 / M_SCALE)
            shares[pl.ds(S * at, S), :] = (
                jnp.concatenate([upper(packed), lower(packed)], axis=0) * unit
            )
        return 0

    lax.fori_loop(0, jnp.maximum(pl.cdiv(n, 2 * PAIR_UNROLL), 1), expand, 0)


def advance(pos, vel, noise, word, top):
    wind = word * (1.0 / W_SCALE) - W_TOP
    fresh = DECAY * vel + KICK * noise
    return fresh, jnp.clip(pos + STEP * (wind + fresh), 0.0, top)


def take_up(places, box, z_rows):
    def take(b, _):
        z_rows[pl.ds(b, 1), :] = lax.shift_right_logical(
            box[pl.ds(places[3, b], 1), :], jnp.full((1, BLK), places[4, b], jnp.int32)
        )
        return 0

    lax.fori_loop(0, z_rows.shape[0], take, 0, unroll=8)
    return lower(z_rows[...])


def height_kernel(places, pairs, box, pos, vel, noise, keys, out, z_rows):
    up = take_up(places, box, z_rows)
    _, height = advance(pos[2], vel[2], noise[2], up, LEV - 1.0)
    z_rows[...] = (keys[...] << 16) | fixed(height, LEV_SCALE)

    def put(b, _):
        out[pl.ds(places[5, b], 1), :] = z_rows[pl.ds(b, 1), :]
        return 0

    lax.fori_loop(0, z_rows.shape[0], put, 0, unroll=8)


def move_kernel(places, box, pos, vel, noise, moved, turb, yx_rows, z_rows):
    def take(b, _):
        yx_rows[pl.ds(b, 1), :] = box[pl.ds(places[2, b], 1), :]
        return 0

    lax.fori_loop(0, yx_rows.shape[0], take, 0, unroll=8)
    yx = yx_rows[...]
    words = (upper(yx), lower(yx), take_up(places, box, z_rows))
    for c, top in enumerate((BY - 1.0, BX - 1.0, LEV - 1.0)):
        turb[c], moved[c] = advance(pos[c], vel[c], noise[c], words[c], top)


def deposit_kernel(items, homes, pairs, box, shares, out, total, sems):
    n = pairs[0]
    total[...] = jnp.zeros(total.shape, jnp.float32)
    level = lax.broadcasted_iota(jnp.int32, (8, BLK), 0).astype(jnp.float32)
    cells = lax.broadcasted_iota(jnp.int32, (MBC, BLK), 0).astype(jnp.float32)
    cells = cells.astype(jnp.bfloat16)
    one, none = jnp.bfloat16(1), jnp.bfloat16(0)

    def step(i, done):
        for j in range(PAIR_UNROLL):
            pair = i * PAIR_UNROLL + j
            weights, picks = [], []
            for half in range(2):
                at = 2 * pair + half
                row = jnp.maximum(items[at], 0)
                word = box[pl.ds(row, 1), :]
                height = jnp.broadcast_to(lower(word) * (1.0 / LEV_SCALE), (8, BLK))
                vert = [hat(height - (level + 8.0 * k)) for k in range(LEV // 8)]
                held = [
                    shares[pl.ds(S * at + s, 8, stride=0), :] * part for s in range(S) for part in vert
                ]
                weights.append(jnp.concatenate(held, axis=0).astype(jnp.bfloat16))
                cell = (word >> 16) & (MBC - 1)
                cell = cell.astype(jnp.float32).astype(jnp.bfloat16)
                picks.append(jnp.where(cells == cell, one, none))
            part = lax.dot_general(
                jnp.concatenate(weights, axis=1),
                jnp.concatenate(picks, axis=1),
                (((1,), (1,)), ((), ())),
                preferred_element_type=jnp.float32,
            )
            home = homes[pair]
            total[home] = total[home] + part
        later = (i + 1) * PAIR_UNROLL
        final = jnp.where(later < n, homes[later], MB)

        def leave(h, _):
            pltpu.make_async_copy(total.at[h], out.at[h], sems.at[h]).start()
            return 0

        lax.fori_loop(done, final, leave, 0)
        return final

    steps = jnp.maximum(pl.cdiv(n, PAIR_UNROLL), 1)
    lax.fori_loop(0, steps, step, jnp.int32(0))
    for h in range(MB):
        pltpu.make_async_copy(total.at[h], out.at[h], sems.at[h]).wait()


def swap(box, devices):
    rows = box.shape[0] // devices
    step = 8 if rows % 8 == 0 else 2 if rows % 2 == 0 else 1
    whole_box = box.reshape(devices * rows // step, step, BLK)
    arrived = lax.all_to_all(whole_box, AXES, split_axis=0, concat_axis=0, tiled=True)
    return arrived.reshape(box.shape)


def body(
    winds, positions, velocity, increments, mass, requests, block_slots, destinations, cell_keys
):
    devices = lax.axis_size("lat") * lax.axis_size("lon")
    blocks = positions.shape[0]
    params = pltpu.CompilerParams(vmem_limit_bytes=40 << 20)
    smem, vmem, hbm = whole(pltpu.SMEM), whole(), whole(pltpu.HBM)
    i32, f32 = jnp.int32, jnp.float32
    dma = pltpu.SemaphoreType.DMA
    notes = [pltpu.VMEM((8, devices), i32), pltpu.SMEM((8, devices), i32)]
    by_part = (1, 0, 2)
    pos = positions.transpose(by_part)
    stay = lambda x: pltpu.with_memory_space_constraint(x, pltpu.HBM)
    box, places = pl.pallas_call(
        pack_kernel,
        name="pack",
        out_shape=(
            jax.ShapeDtypeStruct((devices * ROWS, BLK), i32),
            jax.ShapeDtypeStruct((8, blocks), i32),
        ),
        in_specs=[hbm] * 6,
        out_specs=(vmem, smem),
        scratch_shapes=[
            pltpu.VMEM((1, blocks), i32),
            pltpu.VMEM((Q, devices), i32),
            pltpu.VMEM((1, blocks), i32),
            pltpu.VMEM((blocks, BLK), i32),
            pltpu.VMEM((3, blocks, BLK), f32),
            pltpu.VMEM((blocks, S, BLK), f32),
            pltpu.VMEM((2 * blocks, BLK), i32),
            pltpu.VMEM((8, blocks), i32),
            dma((7,)),
        ],
        compiler_params=params,
    )(
        stay(block_slots.transpose(1, 0)),
        stay(requests.reshape(devices, Q).transpose(1, 0)),
        stay(destinations.transpose(1, 0)),
        stay(cell_keys),
        stay(pos),
        stay(mass),
    )
    box = swap(box, devices)
    local_wind = pl.pallas_call(
        sample_kernel,
        name="sample",
        out_shape=jax.ShapeDtypeStruct((devices * WIND_ROWS, BLK), i32),
        in_specs=[vmem, vmem],
        out_specs=vmem,
        scratch_shapes=[
            pltpu.SMEM((devices * ROOM + ROOM,), i32),
            pltpu.VMEM((devices * 2 * ROOM, BLK), i32),
            *notes,
            dma,
        ],
        compiler_params=params,
    )(box, winds.reshape(MB, 3 * LEV, MBC))
    room = devices * CAP + MB + 2 * PAIR_UNROLL
    items, homes, pairs, shares = pl.pallas_call(
        order_kernel,
        name="order",
        cost_estimate=pl.CostEstimate(flops=10**9, bytes_accessed=20 << 20, transcendentals=0),
        out_shape=(
            jax.ShapeDtypeStruct((room + devices * CAP,), i32),
            jax.ShapeDtypeStruct(((room + devices * CAP) // 2 + 1,), i32),
            jax.ShapeDtypeStruct((8,), i32),
            jax.ShapeDtypeStruct((room * S, BLK), f32),
        ),
        in_specs=[vmem],
        out_specs=(smem, smem, smem, vmem),
        scratch_shapes=[
            *notes,
            pltpu.SMEM((MB + 1,), i32),
            pltpu.SMEM((MB + 1,), i32),
            dma,
        ],
        compiler_params=params,
    )(box)
    returned = swap(local_wind, devices)
    drift = (pos, velocity.transpose(by_part), increments.transpose(by_part))
    row_scratch = pltpu.VMEM((blocks, BLK), i32)
    outbox = pl.pallas_call(
        height_kernel,
        name="height",
        out_shape=jax.ShapeDtypeStruct((devices * CAP, BLK), i32),
        in_specs=[smem, smem] + [vmem] * 5,
        out_specs=vmem,
        scratch_shapes=[row_scratch],
        compiler_params=params,
    )(
        places,
        pairs,
        returned,
        *drift,
        cell_keys,
    )
    inbox = swap(outbox, devices)
    moved, turbulence = pl.pallas_call(
        move_kernel,
        name="move",
        out_shape=[jax.ShapeDtypeStruct(pos.shape, f32)] * 2,
        in_specs=[smem] + [vmem] * 4,
        out_specs=[vmem] * 2,
        scratch_shapes=[row_scratch, row_scratch],
        cost_estimate=pl.CostEstimate(flops=10**7, bytes_accessed=2 << 20, transcendentals=0),
        compiler_params=params,
    )(places, returned, *drift)
    total = pl.pallas_call(
        deposit_kernel,
        name="deposit",
        out_shape=jax.ShapeDtypeStruct((MB, S * LEV, MBC), f32),
        in_specs=[smem, smem, smem, vmem, vmem],
        out_specs=hbm,
        scratch_shapes=[pltpu.VMEM((MB, S * LEV, MBC), f32), dma((MB,))],
        compiler_params=params,
    )(items, homes, pairs, inbox, shares)
    return (
        moved.transpose(by_part),
        turbulence.transpose(by_part),
        total.reshape(winds.shape[:2] + (S, LEV, MBC)),
    )


def solution(mesh):
    rows = P(AXES, None, None)
    pairs = P(AXES, None)
    tiles = P("lat", "lon", None, None, None)
    return jax.shard_map(
        body,
        mesh=mesh,
        in_specs=(tiles, rows, rows, rows, rows, rows, pairs, pairs, pairs),
        out_specs=(rows, rows, tiles),
        check_vma=False,
    )
```

```python
import jax
import jax.numpy as jnp
from jax import lax
from jax.experimental import pallas as pl
from jax.experimental.pallas import tpu as pltpu
from jax.sharding import PartitionSpec as P

BY = 8
BX = 16
MBC = 128
LEV = 40
S = 8
BLK = 128
MB = 16
Q = 2
CAP = 2
ROOM = Q * CAP

DECAY = 0.8
KICK = 0.6
STEP = 0.5

AXES = ("lat", "lon")
LOW16 = 0xFFFF
ROW_SCALE = 65535.0 / (BY - 1)
COL_SCALE = 65535.0 / (BX - 1)
LEV_SCALE = 65535.0 / (LEV - 1)
Z_ONE = float(1 << 22)
W_TOP = 6.1
W_SCALE = 65535.0 / (2 * W_TOP)
M_SCALE = 32767.0
SAMPLE_UNROLL = 12
PAIR_UNROLL = 16

SHARE_ROW = 2 * ROOM
NOTE_ROW = SHARE_ROW + CAP * S // 2
ROWS = NOTE_ROW + 1
WIND_ROWS = ROOM + ROOM // 2
HOME_AT = ROOM
LANDED_AT = HOME_AT + CAP
TAKEN_AT = LANDED_AT + 1
EACH = 8
PLAN = 1024
HOMES_AT = 576
PAIRS_AT = PLAN - 1


def hat(offset):
    return jnp.maximum(0.0, 1.0 - jnp.abs(offset))


def fixed(value, scale, shift=0.0):
    return ((value + shift) * scale + 0.5).astype(jnp.int32)


def upper(word):
    return lax.shift_right_logical(word, jnp.int32(16)).astype(jnp.float32)


def lower(word):
    return (word & LOW16).astype(jnp.float32)


def whole(space=pltpu.VMEM):
    return pl.BlockSpec(memory_space=space)


def read_notes(box, rows, notes, sem):
    devices = notes.shape[1]
    sent = box[pl.ds(NOTE_ROW, devices, stride=ROWS), :].astype(jnp.float32)
    rows[...] = sent.T[0 : notes.shape[0], :].astype(jnp.int32)
    copy = pltpu.make_async_copy(rows, notes, sem)
    copy.start()
    copy.wait()


def pack_kernel(
    slots_hbm, asked_hbm, targets_hbm, keys_hbm, pos_hbm, mass_hbm,
    box, places,
    slots, asked, targets, keys, pos, mass, spots, ranks, sems,
):
    blocks, devices = mass.shape[0], asked.shape[1]
    copies = [
        pltpu.make_async_copy(src, dst, sems.at[i])
        for i, (src, dst) in enumerate(
            (
                (slots_hbm, slots),
                (targets_hbm, targets),
                (asked_hbm, asked),
                (keys_hbm, keys),
                (pos_hbm, pos),
                (mass_hbm, mass),
            )
        )
    ]
    for copy in copies:
        copy.start()
    square = (blocks, blocks)
    down = lax.broadcasted_iota(jnp.int32, square, 0)
    along = lax.broadcasted_iota(jnp.int32, square, 1)

    def stand(row):
        return jnp.broadcast_to(row.astype(jnp.float32), square).T.astype(jnp.int32)

    def rank(row):
        same = (stand(row) == row) & (down < along)
        return jnp.sum(jnp.where(same, 1.0, 0.0), axis=0, keepdims=True).astype(jnp.int32)

    copies[0].wait()
    slot = slots[...]
    tile = slot // Q
    order = rank(tile)
    lons = lax.axis_size("lon")
    core = (tile // lons) % 2
    helper = (order + lax.axis_index("lat") + lax.axis_index("lon")) % 2
    host = tile + (helper - core) * lons
    seat = core * (ROOM // 2) + order // 2
    copies[1].wait()
    target = targets[...]
    turn = rank(target)
    ranks[0:1, :] = host * ROWS + 2 * seat
    ranks[1:2, :] = target * ROWS + SHARE_ROW + turn * (S // 2)
    ranks[2:3, :] = host * WIND_ROWS + seat
    ranks[3:4, :] = host * WIND_ROWS + ROOM + seat // 2
    ranks[4:5, :] = 16 - 16 * (seat % 2)
    ranks[5:6, :] = target * CAP + turn
    ranked = pltpu.make_async_copy(ranks, places, sems.at[len(copies)])
    ranked.start()
    slot_down = stand(slot)
    tile_down = slot_down // Q
    copies[2].wait()
    met = jnp.where(slot_down % Q == 0, asked[0:1, :], asked[1:2, :])
    met = jnp.where(tile_down == along, met, 0).astype(jnp.float32)
    met = jnp.sum(met, axis=1, keepdims=True)
    met = met + jnp.where(stand(helper) == stand(core), 0.0, float(MB))
    copies[3].wait()
    home = (keys[:, 0:1] // MBC).astype(jnp.float32)
    said = jnp.where(along == stand(seat), met, 0.0)
    said = jnp.where(along == TAKEN_AT, jnp.where(stand(core) == 0, 1.0, float(EACH)), said)
    more = jnp.where(along == HOME_AT + stand(turn), home, 0.0) + jnp.where(
        along == LANDED_AT, 1.0, 0.0
    )
    mine = jnp.concatenate([down == host, down == target], axis=1)
    notes = jnp.dot(
        jnp.where(mine, 1.0, 0.0).astype(jnp.bfloat16),
        jnp.concatenate([said, more], axis=0).astype(jnp.bfloat16),
        preferred_element_type=jnp.float32,
    )
    box[pl.ds(NOTE_ROW, devices, stride=ROWS), :] = notes.astype(jnp.int32)
    copies[4].wait()
    spots[pl.ds(0, blocks, stride=2), :] = (fixed(pos[0], ROW_SCALE) << 16) | fixed(
        pos[1], COL_SCALE
    )
    spots[pl.ds(1, blocks, stride=2), :] = (pos[2] * Z_ONE).astype(jnp.int32)
    copies[5].wait()
    ranked.wait()

    def put(b, _):
        box[pl.ds(places[0, b], 2), :] = spots[pl.ds(2 * b, 2), :]
        share = fixed(mass[b], M_SCALE)
        box[pl.ds(places[1, b], S // 2), :] = (share[0 : S // 2] << 16) | share[S // 2 :]
        return 0

    lax.fori_loop(0, blocks, put, 0, unroll=8)


def sample_kernel(box, winds, out, queue, found, rows, notes, sem):
    devices = notes.shape[1]
    read_notes(box, rows, notes, sem)

    def enlist(t, n):
        taken = notes[TAKEN_AT, t]
        for r in range(ROOM // 2):
            queue[n + r] = t * ROOM + r
        n = n + taken % EACH
        for r in range(ROOM // 2):
            queue[n + r] = t * ROOM + ROOM // 2 + r
        return n + taken // EACH

    n = lax.fori_loop(0, devices, enlist, 0, unroll=4)
    levels = lax.broadcasted_iota(jnp.int32, (LEV, BLK), 0).astype(jnp.float32)
    lats = lax.broadcasted_iota(jnp.int32, (BY, BLK), 0).astype(jnp.float32)
    lons = lax.broadcasted_iota(jnp.int32, (BX, BLK), 0).astype(jnp.float32)

    def step(i, _):
        for j in range(SAMPLE_UNROLL):
            item = queue[jnp.minimum(i * SAMPLE_UNROLL + j, n - 1)]
            row = (item // ROOM) * ROWS + 2 * (item % ROOM)
            yx = box[pl.ds(row, 1), :]
            height = box[pl.ds(row + 1, 1), :]
            hy = hat(upper(yx) * (1.0 / ROW_SCALE) - lats)
            hx = hat(lower(yx) * (1.0 / COL_SCALE) - lons)
            wz = hat(height.astype(jnp.float32) * (1.0 / Z_ONE) - levels)
            wz = wz.astype(jnp.bfloat16).astype(jnp.float32)
            flat = (hy[:, None, :] * hx[None, :, :]).reshape(MBC, BLK)
            high = flat.astype(jnp.bfloat16)
            low = (flat - high.astype(jnp.float32)).astype(jnp.bfloat16)
            met = winds[notes[item % ROOM, item // ROOM]]
            level_wind = jnp.dot(met, high, preferred_element_type=jnp.float32) + jnp.dot(
                met, low, preferred_element_type=jnp.float32
            )
            wind = [
                jnp.sum(level_wind[c * LEV : (c + 1) * LEV] * wz, axis=0, keepdims=True)
                for c in range(3)
            ]
            found[pl.ds(2 * item, 1), :] = (fixed(wind[0], W_SCALE, W_TOP) << 16) | fixed(
                wind[1], W_SCALE, W_TOP
            )
            found[pl.ds(2 * item + 1, 1), :] = fixed(wind[2], W_SCALE, W_TOP)
        return 0

    lax.fori_loop(0, pl.cdiv(n, SAMPLE_UNROLL), step, 0)

    def every(r):
        return found[pl.ds(r, devices, stride=2 * ROOM), :]

    for r in range(ROOM):
        out[pl.ds(r, devices, stride=WIND_ROWS), :] = every(2 * r)
    for r in range(0, ROOM, 2):
        out[pl.ds(ROOM + r // 2, devices, stride=WIND_ROWS), :] = (every(2 * r + 1) << 16) | (
            every(2 * r + 3) & LOW16
        )


def order_kernel(box, plan, shares, rows, notes, starts, tally, sem):
    devices = notes.shape[1]
    read_notes(box, rows, notes, sem)

    room = shares.shape[0] // S

    def clear(i, _):
        plan[i] = -1
        return 0

    lax.fori_loop(0, room, clear, 0, unroll=8)

    def clear_home(i, _):
        plan[HOMES_AT + i] = 0
        return 0

    lax.fori_loop(0, room // 2, clear_home, 0, unroll=8)
    for h in range(MB):
        tally[h] = 0

    def tell(t, _):
        landed = notes[LANDED_AT, t]
        for r in range(CAP):
            home = jnp.where(r < landed, notes[HOME_AT + r, t], MB)
            tally[home] = tally[home] + 1
        return 0

    tally[MB] = 0
    lax.fori_loop(0, devices, tell, 0, unroll=4)
    n = jnp.int32(0)
    for h in range(MB):
        starts[h] = n
        n = n + (tally[h] + 1) // 2 * 2
    starts[MB] = room

    def place(t, _):
        landed = notes[LANDED_AT, t]
        for r in range(CAP):
            there = r < landed
            home = jnp.where(there, notes[HOME_AT + r, t], MB)
            at = starts[home]
            starts[home] = at + 1
            plan[at] = jnp.where(there, t * CAP + r, -1)
            plan[HOMES_AT + at // 2] = jnp.where(there, home, 0)
        return 0

    lax.fori_loop(0, devices, place, 0, unroll=4)
    plan[PAIRS_AT] = n // 2

    def expand(i, _):
        for j in range(2 * PAIR_UNROLL):
            at = i * 2 * PAIR_UNROLL + j
            item = plan[at]
            row = jnp.maximum(item, 0)
            packed = box[pl.ds((row // CAP) * ROWS + SHARE_ROW + (row % CAP) * (S // 2), S // 2), :]
            unit = jnp.where(item < 0, 0.0, 1.0 / M_SCALE)
            shares[pl.ds(S * at, S), :] = (
                jnp.concatenate([upper(packed), lower(packed)], axis=0) * unit
            )
        return 0

    lax.fori_loop(0, jnp.maximum(pl.cdiv(n, 2 * PAIR_UNROLL), 1), expand, 0)


def advance(pos, vel, noise, word, top):
    wind = word * (1.0 / W_SCALE) - W_TOP
    fresh = DECAY * vel + KICK * noise
    return fresh, jnp.clip(pos + STEP * (wind + fresh), 0.0, top)


def take_up(places, box, z_rows):
    def take(b, _):
        z_rows[pl.ds(b, 1), :] = lax.shift_right_logical(
            box[pl.ds(places[3, b], 1), :], jnp.full((1, BLK), places[4, b], jnp.int32)
        )
        return 0

    lax.fori_loop(0, z_rows.shape[0], take, 0, unroll=8)
    return lower(z_rows[...])


def height_kernel(places, plan, box, pos, vel, noise, keys, out, z_rows):
    up = take_up(places, box, z_rows)
    _, height = advance(pos[2], vel[2], noise[2], up, LEV - 1.0)
    z_rows[...] = (keys[...] << 16) | fixed(height, LEV_SCALE)

    def put(b, _):
        out[pl.ds(places[5, b], 1), :] = z_rows[pl.ds(b, 1), :]
        return 0

    lax.fori_loop(0, z_rows.shape[0], put, 0, unroll=8)


def move_kernel(places, box, pos, vel, noise, moved, turb, yx_rows, z_rows):
    def take(b, _):
        yx_rows[pl.ds(b, 1), :] = box[pl.ds(places[2, b], 1), :]
        return 0

    lax.fori_loop(0, yx_rows.shape[0], take, 0, unroll=8)
    yx = yx_rows[...]
    words = (upper(yx), lower(yx), take_up(places, box, z_rows))
    for c, top in enumerate((BY - 1.0, BX - 1.0, LEV - 1.0)):
        turb[c], moved[c] = advance(pos[c], vel[c], noise[c], words[c], top)


def deposit_kernel(plan, box, shares, out, total, sems):
    n = plan[PAIRS_AT]
    total[...] = jnp.zeros(total.shape, jnp.float32)
    level = lax.broadcasted_iota(jnp.int32, (8, BLK), 0).astype(jnp.float32)
    cells = lax.broadcasted_iota(jnp.int32, (MBC, BLK), 0).astype(jnp.float32)
    cells = cells.astype(jnp.bfloat16)
    one, none = jnp.bfloat16(1), jnp.bfloat16(0)

    def step(i, done):
        for j in range(PAIR_UNROLL):
            pair = i * PAIR_UNROLL + j
            weights, picks = [], []
            for half in range(2):
                at = 2 * pair + half
                row = jnp.maximum(plan[at], 0)
                word = box[pl.ds(row, 1), :]
                height = jnp.broadcast_to(lower(word) * (1.0 / LEV_SCALE), (8, BLK))
                vert = [hat(height - (level + 8.0 * k)) for k in range(LEV // 8)]
                held = [
                    shares[pl.ds(S * at + s, 8, stride=0), :] * part for s in range(S) for part in vert
                ]
                weights.append(jnp.concatenate(held, axis=0).astype(jnp.bfloat16))
                cell = (word >> 16) & (MBC - 1)
                cell = cell.astype(jnp.float32).astype(jnp.bfloat16)
                picks.append(jnp.where(cells == cell, one, none))
            part = lax.dot_general(
                jnp.concatenate(weights, axis=1),
                jnp.concatenate(picks, axis=1),
                (((1,), (1,)), ((), ())),
                preferred_element_type=jnp.float32,
            )
            home = plan[HOMES_AT + pair]
            total[home] = total[home] + part
        later = (i + 1) * PAIR_UNROLL
        final = jnp.where(later < n, plan[HOMES_AT + later], MB)

        def leave(h, _):
            pltpu.make_async_copy(total.at[h], out.at[h], sems.at[h]).start()
            return 0

        lax.fori_loop(done, final, leave, 0)
        return final

    steps = jnp.maximum(pl.cdiv(n, PAIR_UNROLL), 1)
    lax.fori_loop(0, steps, step, jnp.int32(0))
    for h in range(MB):
        pltpu.make_async_copy(total.at[h], out.at[h], sems.at[h]).wait()


def swap(box, devices):
    rows = box.shape[0] // devices
    step = 8 if rows % 8 == 0 else 2 if rows % 2 == 0 else 1
    whole_box = box.reshape(devices * rows // step, step, BLK)
    arrived = lax.all_to_all(whole_box, AXES, split_axis=0, concat_axis=0, tiled=True)
    return arrived.reshape(box.shape)


def body(
    winds, positions, velocity, increments, mass, requests, block_slots, destinations, cell_keys
):
    devices = lax.axis_size("lat") * lax.axis_size("lon")
    blocks = positions.shape[0]
    params = pltpu.CompilerParams(vmem_limit_bytes=40 << 20)
    smem, vmem, hbm = whole(pltpu.SMEM), whole(), whole(pltpu.HBM)
    i32, f32 = jnp.int32, jnp.float32
    dma = pltpu.SemaphoreType.DMA
    notes = [pltpu.VMEM((8, devices), i32), pltpu.SMEM((8, devices), i32)]
    by_part = (1, 0, 2)
    pos = positions.transpose(by_part)
    stay = lambda x: pltpu.with_memory_space_constraint(x, pltpu.HBM)
    others = lax.ppermute(winds, "lat", [(i, i ^ 1) for i in range(lax.axis_size("lat"))])
    both = jnp.stack([winds, others]).reshape(2 * MB, 3 * LEV, MBC)
    box, places = pl.pallas_call(
        pack_kernel,
        name="pack",
        out_shape=(
            jax.ShapeDtypeStruct((devices * ROWS, BLK), i32),
            jax.ShapeDtypeStruct((8, blocks), i32),
        ),
        in_specs=[hbm] * 6,
        out_specs=(vmem, smem),
        scratch_shapes=[
            pltpu.VMEM((1, blocks), i32),
            pltpu.VMEM((Q, devices), i32),
            pltpu.VMEM((1, blocks), i32),
            pltpu.VMEM((blocks, BLK), i32),
            pltpu.VMEM((3, blocks, BLK), f32),
            pltpu.VMEM((blocks, S, BLK), f32),
            pltpu.VMEM((2 * blocks, BLK), i32),
            pltpu.VMEM((8, blocks), i32),
            dma((7,)),
        ],
        compiler_params=params,
    )(
        stay(block_slots.transpose(1, 0)),
        stay(requests.reshape(devices, Q).transpose(1, 0)),
        stay(destinations.transpose(1, 0)),
        stay(cell_keys),
        stay(pos),
        stay(mass),
    )
    box = swap(box, devices)
    local_wind = pl.pallas_call(
        sample_kernel,
        name="sample",
        out_shape=jax.ShapeDtypeStruct((devices * WIND_ROWS, BLK), i32),
        in_specs=[vmem] * 2,
        out_specs=vmem,
        scratch_shapes=[
            pltpu.SMEM((devices * ROOM + ROOM,), i32),
            pltpu.VMEM((devices * 2 * ROOM, BLK), i32),
            *notes,
            dma,
        ],
        compiler_params=params,
    )(box, both)
    room = devices * CAP + MB + 2 * PAIR_UNROLL
    assert room + devices * CAP <= HOMES_AT and HOMES_AT + (room + devices * CAP) // 2 < PAIRS_AT
    plan, shares = pl.pallas_call(
        order_kernel,
        name="order",
        cost_estimate=pl.CostEstimate(flops=10**9, bytes_accessed=20 << 20, transcendentals=0),
        out_shape=(
            jax.ShapeDtypeStruct((PLAN,), i32),
            jax.ShapeDtypeStruct((room * S, BLK), f32),
        ),
        in_specs=[vmem],
        out_specs=(smem, vmem),
        scratch_shapes=[
            *notes,
            pltpu.SMEM((MB + 1,), i32),
            pltpu.SMEM((MB + 1,), i32),
            dma,
        ],
        compiler_params=params,
    )(box)
    returned = swap(local_wind, devices)
    drift = (pos, velocity.transpose(by_part), increments.transpose(by_part))
    row_scratch = pltpu.VMEM((blocks, BLK), i32)
    outbox = pl.pallas_call(
        height_kernel,
        name="height",
        out_shape=jax.ShapeDtypeStruct((devices * CAP, BLK), i32),
        in_specs=[smem, whole(pl.ANY)] + [vmem] * 5,
        out_specs=vmem,
        scratch_shapes=[row_scratch],
        compiler_params=params,
    )(
        places,
        plan,
        returned,
        *drift,
        cell_keys,
    )
    inbox = swap(outbox, devices)
    moved, turbulence = pl.pallas_call(
        move_kernel,
        name="move",
        out_shape=[jax.ShapeDtypeStruct(pos.shape, f32)] * 2,
        in_specs=[smem] + [vmem] * 4,
        out_specs=[vmem] * 2,
        scratch_shapes=[row_scratch, row_scratch],
        cost_estimate=pl.CostEstimate(flops=10**7, bytes_accessed=2 << 20, transcendentals=0),
        compiler_params=params,
    )(places, returned, *drift)
    total = pl.pallas_call(
        deposit_kernel,
        name="deposit",
        out_shape=jax.ShapeDtypeStruct((MB, S * LEV, MBC), f32),
        in_specs=[smem, vmem, vmem],
        out_specs=hbm,
        scratch_shapes=[pltpu.VMEM((MB, S * LEV, MBC), f32), dma((MB,))],
        compiler_params=params,
    )(plan, inbox, shares)
    return (
        moved.transpose(by_part),
        turbulence.transpose(by_part),
        total.reshape(winds.shape[:2] + (S, LEV, MBC)),
    )


def solution(mesh):
    rows = P(AXES, None, None)
    pairs = P(AXES, None)
    tiles = P("lat", "lon", None, None, None)
    return jax.shard_map(
        body,
        mesh=mesh,
        in_specs=(tiles, rows, rows, rows, rows, rows, pairs, pairs, pairs),
        out_specs=(rows, rows, tiles),
        check_vma=False,
    )
```

```python
import jax
import jax.numpy as jnp
from jax import lax
from jax.experimental import pallas as pl
from jax.experimental.pallas import tpu as pltpu
from jax.sharding import PartitionSpec as P

BY = 8
BX = 16
MBC = 128
LEV = 40
S = 8
BLK = 128
MB = 16
Q = 2
CAP = 2
ROOM = Q * CAP

DECAY = 0.8
KICK = 0.6
STEP = 0.5

AXES = ("lat", "lon")
LOW16 = 0xFFFF
ROW_SCALE = 65535.0 / (BY - 1)
COL_SCALE = 65535.0 / (BX - 1)
LEV_SCALE = 65535.0 / (LEV - 1)
Z_ONE = float(1 << 22)
W_TOP = 6.1
W_SCALE = 65535.0 / (2 * W_TOP)
M_SCALE = 32767.0
SAMPLE_UNROLL = 12
PAIR_UNROLL = 16

SHARE_ROW = 2 * ROOM
NOTE_ROW = SHARE_ROW + CAP * S // 2
ROWS = NOTE_ROW + 1
WIND_ROWS = ROOM + ROOM // 2
HOME_AT = ROOM
LANDED_AT = HOME_AT + CAP
TAKEN_AT = LANDED_AT + 1
EACH = 8
PLAN = 1024
HOMES_AT = 576
PAIRS_AT = PLAN - 1


def hat(offset):
    return jnp.maximum(0.0, 1.0 - jnp.abs(offset))


def fixed(value, scale, shift=0.0):
    return ((value + shift) * scale + 0.5).astype(jnp.int32)


def upper(word):
    return lax.shift_right_logical(word, jnp.int32(16)).astype(jnp.float32)


def lower(word):
    return (word & LOW16).astype(jnp.float32)


def whole(space=pltpu.VMEM):
    return pl.BlockSpec(memory_space=space)


def read_notes(box, rows, notes, sem):
    devices = notes.shape[1]
    sent = box[pl.ds(NOTE_ROW, devices, stride=ROWS), :].astype(jnp.float32)
    rows[...] = sent.T[0 : notes.shape[0], :].astype(jnp.int32)
    copy = pltpu.make_async_copy(rows, notes, sem)
    copy.start()
    copy.wait()


def pack_kernel(
    slots_hbm, asked_hbm, targets_hbm, keys_hbm, pos_hbm, mass_hbm,
    box, places,
    slots, asked, targets, keys, pos, mass, spots, ranks, sems,
):
    blocks, devices = mass.shape[0], asked.shape[1]
    copies = [
        pltpu.make_async_copy(src, dst, sems.at[i])
        for i, (src, dst) in enumerate(
            (
                (slots_hbm, slots),
                (targets_hbm, targets),
                (asked_hbm, asked),
                (keys_hbm, keys),
                (pos_hbm, pos),
                (mass_hbm, mass),
            )
        )
    ]
    for copy in copies:
        copy.start()
    square = (blocks, blocks)
    down = lax.broadcasted_iota(jnp.int32, square, 0)
    along = lax.broadcasted_iota(jnp.int32, square, 1)

    def stand(row):
        return jnp.broadcast_to(row.astype(jnp.float32), square).T.astype(jnp.int32)

    def rank(row):
        same = (stand(row) == row) & (down < along)
        return jnp.sum(jnp.where(same, 1.0, 0.0), axis=0, keepdims=True).astype(jnp.int32)

    copies[0].wait()
    slot = slots[...]
    tile = slot >> 1
    order = rank(tile)
    lons = lax.axis_size("lon")
    core = (tile >> (lons.bit_length() - 1)) & 1
    helper = (order + lax.axis_index("lat") + lax.axis_index("lon")) & 1
    host = tile + (helper - core) * lons
    seat = core * (ROOM // 2) + (order >> 1)
    copies[1].wait()
    target = targets[...]
    turn = rank(target)
    ranks[0:1, :] = host * ROWS + 2 * seat
    ranks[1:2, :] = target * ROWS + SHARE_ROW + turn * (S // 2)
    ranks[2:3, :] = host * WIND_ROWS + seat
    ranks[3:4, :] = host * WIND_ROWS + ROOM + (seat >> 1)
    ranks[4:5, :] = 16 - 16 * (seat & 1)
    ranks[5:6, :] = target * CAP + turn
    ranked = pltpu.make_async_copy(ranks, places, sems.at[len(copies)])
    ranked.start()
    bits = stand((turn << 15) | (seat << 13) | (helper << 12) | slot)
    slot_down = bits & 0xFFF
    helper_down = (bits >> 12) & 1
    seat_down = (bits >> 13) & (ROOM - 1)
    turn_down = bits >> 15
    core_down = seat_down >> 1
    copies[2].wait()
    met = jnp.where((slot_down & 1) == 0, asked[0:1, :], asked[1:2, :])
    met = jnp.where((slot_down >> 1) == along, met, 0).astype(jnp.float32)
    met = jnp.sum(met, axis=1, keepdims=True)
    met = met + jnp.where(helper_down == core_down, 0.0, float(MB))
    copies[3].wait()
    home = (keys[:, 0:1] >> 7).astype(jnp.float32)
    said = jnp.where(along == seat_down, met, 0.0)
    said = jnp.where(along == TAKEN_AT, jnp.where(core_down == 0, 1.0, float(EACH)), said)
    more = jnp.where(along == HOME_AT + turn_down, home, 0.0) + jnp.where(
        along == LANDED_AT, 1.0, 0.0
    )
    mine = jnp.concatenate([down == host, down == target], axis=1)
    notes = jnp.dot(
        jnp.where(mine, 1.0, 0.0).astype(jnp.bfloat16),
        jnp.concatenate([said, more], axis=0).astype(jnp.bfloat16),
        preferred_element_type=jnp.float32,
    )
    box[pl.ds(NOTE_ROW, devices, stride=ROWS), :] = notes.astype(jnp.int32)
    copies[4].wait()
    spots[pl.ds(0, blocks, stride=2), :] = (fixed(pos[0], ROW_SCALE) << 16) | fixed(
        pos[1], COL_SCALE
    )
    spots[pl.ds(1, blocks, stride=2), :] = (pos[2] * Z_ONE).astype(jnp.int32)
    copies[5].wait()
    ranked.wait()

    def put(b, _):
        box[pl.ds(places[0, b], 2), :] = spots[pl.ds(2 * b, 2), :]
        share = fixed(mass[b], M_SCALE)
        box[pl.ds(places[1, b], S // 2), :] = (share[0 : S // 2] << 16) | share[S // 2 :]
        return 0

    lax.fori_loop(0, blocks, put, 0, unroll=8)


def sample_kernel(box, winds, out, queue, found, rows, notes, sem):
    devices = notes.shape[1]
    read_notes(box, rows, notes, sem)

    def enlist(t, n):
        taken = notes[TAKEN_AT, t]
        for r in range(ROOM // 2):
            queue[n + r] = t * ROOM + r
        n = n + (taken & (EACH - 1))
        for r in range(ROOM // 2):
            queue[n + r] = t * ROOM + ROOM // 2 + r
        return n + (taken >> 3)

    n = lax.fori_loop(0, devices, enlist, 0, unroll=4)
    levels = lax.broadcasted_iota(jnp.int32, (LEV, BLK), 0).astype(jnp.float32)
    lats = lax.broadcasted_iota(jnp.int32, (BY, BLK), 0).astype(jnp.float32)
    lons = lax.broadcasted_iota(jnp.int32, (BX, BLK), 0).astype(jnp.float32)

    def step(i, _):
        for j in range(SAMPLE_UNROLL):
            item = queue[jnp.minimum(i * SAMPLE_UNROLL + j, n - 1)]
            src, seat = item >> 2, item & (ROOM - 1)
            row = src * ROWS + 2 * seat
            yx = box[pl.ds(row, 1), :]
            height = box[pl.ds(row + 1, 1), :]
            hy = hat(upper(yx) * (1.0 / ROW_SCALE) - lats)
            hx = hat(lower(yx) * (1.0 / COL_SCALE) - lons)
            wz = hat(height.astype(jnp.float32) * (1.0 / Z_ONE) - levels)
            wz = wz.astype(jnp.bfloat16).astype(jnp.float32)
            flat = (hy[:, None, :] * hx[None, :, :]).reshape(MBC, BLK)
            high = flat.astype(jnp.bfloat16)
            low = (flat - high.astype(jnp.float32)).astype(jnp.bfloat16)
            met = winds[notes[seat, src]]
            level_wind = jnp.dot(met, high, preferred_element_type=jnp.float32) + jnp.dot(
                met, low, preferred_element_type=jnp.float32
            )
            wind = [
                jnp.sum(level_wind[c * LEV : (c + 1) * LEV] * wz, axis=0, keepdims=True)
                for c in range(3)
            ]
            found[pl.ds(2 * item, 1), :] = (fixed(wind[0], W_SCALE, W_TOP) << 16) | fixed(
                wind[1], W_SCALE, W_TOP
            )
            found[pl.ds(2 * item + 1, 1), :] = fixed(wind[2], W_SCALE, W_TOP)
        return 0

    lax.fori_loop(0, pl.cdiv(n, SAMPLE_UNROLL), step, 0)

    def every(r):
        return found[pl.ds(r, devices, stride=2 * ROOM), :]

    for r in range(ROOM):
        out[pl.ds(r, devices, stride=WIND_ROWS), :] = every(2 * r)
    for r in range(0, ROOM, 2):
        out[pl.ds(ROOM + r // 2, devices, stride=WIND_ROWS), :] = (every(2 * r + 1) << 16) | (
            every(2 * r + 3) & LOW16
        )


def order_kernel(box, plan, shares, rows, notes, starts, tally, sem):
    devices = notes.shape[1]
    read_notes(box, rows, notes, sem)

    room = shares.shape[0] // S

    def clear(i, _):
        plan[i] = -1
        return 0

    lax.fori_loop(0, room, clear, 0, unroll=8)

    def clear_home(i, _):
        plan[HOMES_AT + i] = 0
        return 0

    lax.fori_loop(0, room // 2, clear_home, 0, unroll=8)
    for h in range(MB):
        tally[h] = 0

    def tell(t, _):
        landed = notes[LANDED_AT, t]
        for r in range(CAP):
            home = jnp.where(r < landed, notes[HOME_AT + r, t], MB)
            tally[home] = tally[home] + 1
        return 0

    tally[MB] = 0
    lax.fori_loop(0, devices, tell, 0, unroll=4)
    n = jnp.int32(0)
    for h in range(MB):
        starts[h] = n
        n = n + ((tally[h] + 1) & ~1)
    starts[MB] = room

    def place(t, _):
        landed = notes[LANDED_AT, t]
        for r in range(CAP):
            there = r < landed
            home = jnp.where(there, notes[HOME_AT + r, t], MB)
            at = starts[home]
            starts[home] = at + 1
            plan[at] = jnp.where(there, t * CAP + r, -1)
            plan[HOMES_AT + (at >> 1)] = jnp.where(there, home, 0)
        return 0

    lax.fori_loop(0, devices, place, 0, unroll=4)
    plan[PAIRS_AT] = n >> 1

    def expand(i, _):
        for j in range(2 * PAIR_UNROLL):
            at = i * 2 * PAIR_UNROLL + j
            item = plan[at]
            row = jnp.maximum(item, 0)
            packed = box[pl.ds((row >> 1) * ROWS + SHARE_ROW + (row & 1) * (S // 2), S // 2), :]
            unit = jnp.where(item < 0, 0.0, 1.0 / M_SCALE)
            shares[pl.ds(S * at, S), :] = (
                jnp.concatenate([upper(packed), lower(packed)], axis=0) * unit
            )
        return 0

    lax.fori_loop(0, jnp.maximum(pl.cdiv(n, 2 * PAIR_UNROLL), 1), expand, 0)


def advance(pos, vel, noise, word, top):
    wind = word * (1.0 / W_SCALE) - W_TOP
    fresh = DECAY * vel + KICK * noise
    return fresh, jnp.clip(pos + STEP * (wind + fresh), 0.0, top)


def take_up(places, box, z_rows):
    def take(b, _):
        z_rows[pl.ds(b, 1), :] = lax.shift_right_logical(
            box[pl.ds(places[3, b], 1), :], jnp.full((1, BLK), places[4, b], jnp.int32)
        )
        return 0

    lax.fori_loop(0, z_rows.shape[0], take, 0, unroll=8)
    return lower(z_rows[...])


def height_kernel(places, plan, box, pos, vel, noise, keys, out, z_rows):
    up = take_up(places, box, z_rows)
    _, height = advance(pos[2], vel[2], noise[2], up, LEV - 1.0)
    z_rows[...] = (keys[...] << 16) | fixed(height, LEV_SCALE)

    def put(b, _):
        out[pl.ds(places[5, b], 1), :] = z_rows[pl.ds(b, 1), :]
        return 0

    lax.fori_loop(0, z_rows.shape[0], put, 0, unroll=8)


def move_kernel(places, box, pos, vel, noise, moved, turb, yx_rows, z_rows):
    def take(b, _):
        yx_rows[pl.ds(b, 1), :] = box[pl.ds(places[2, b], 1), :]
        return 0

    lax.fori_loop(0, yx_rows.shape[0], take, 0, unroll=8)
    yx = yx_rows[...]
    words = (upper(yx), lower(yx), take_up(places, box, z_rows))
    for c, top in enumerate((BY - 1.0, BX - 1.0, LEV - 1.0)):
        turb[c], moved[c] = advance(pos[c], vel[c], noise[c], words[c], top)


def deposit_kernel(plan, box, shares, out, total, sems):
    n = plan[PAIRS_AT]
    total[...] = jnp.zeros(total.shape, jnp.float32)
    level = lax.broadcasted_iota(jnp.int32, (8, BLK), 0).astype(jnp.float32)
    cells = lax.broadcasted_iota(jnp.int32, (MBC, BLK), 0).astype(jnp.float32)
    cells = cells.astype(jnp.bfloat16)
    one, none = jnp.bfloat16(1), jnp.bfloat16(0)

    def step(i, done):
        for j in range(PAIR_UNROLL):
            pair = i * PAIR_UNROLL + j
            weights, picks = [], []
            for half in range(2):
                at = 2 * pair + half
                row = jnp.maximum(plan[at], 0)
                word = box[pl.ds(row, 1), :]
                height = jnp.broadcast_to(lower(word) * (1.0 / LEV_SCALE), (8, BLK))
                vert = [hat(height - (level + 8.0 * k)) for k in range(LEV // 8)]
                held = [
                    shares[pl.ds(S * at + s, 8, stride=0), :] * part for s in range(S) for part in vert
                ]
                weights.append(jnp.concatenate(held, axis=0).astype(jnp.bfloat16))
                cell = (word >> 16) & (MBC - 1)
                cell = cell.astype(jnp.float32).astype(jnp.bfloat16)
                picks.append(jnp.where(cells == cell, one, none))
            part = lax.dot_general(
                jnp.concatenate(weights, axis=1),
                jnp.concatenate(picks, axis=1),
                (((1,), (1,)), ((), ())),
                preferred_element_type=jnp.float32,
            )
            home = plan[HOMES_AT + pair]
            total[home] = total[home] + part
        later = (i + 1) * PAIR_UNROLL
        final = jnp.where(later < n, plan[HOMES_AT + later], MB)

        def leave(h, _):
            pltpu.make_async_copy(total.at[h], out.at[h], sems.at[h]).start()
            return 0

        lax.fori_loop(done, final, leave, 0)
        return final

    steps = jnp.maximum(pl.cdiv(n, PAIR_UNROLL), 1)
    lax.fori_loop(0, steps, step, jnp.int32(0))
    for h in range(MB):
        pltpu.make_async_copy(total.at[h], out.at[h], sems.at[h]).wait()


def swap(box, devices):
    rows = box.shape[0] // devices
    step = 8 if rows % 8 == 0 else 2 if rows % 2 == 0 else 1
    whole_box = box.reshape(devices * rows // step, step, BLK)
    arrived = lax.all_to_all(whole_box, AXES, split_axis=0, concat_axis=0, tiled=True)
    return arrived.reshape(box.shape)


def body(
    winds, positions, velocity, increments, mass, requests, block_slots, destinations, cell_keys
):
    devices = lax.axis_size("lat") * lax.axis_size("lon")
    blocks = positions.shape[0]
    params = pltpu.CompilerParams(vmem_limit_bytes=40 << 20)
    smem, vmem, hbm = whole(pltpu.SMEM), whole(), whole(pltpu.HBM)
    i32, f32 = jnp.int32, jnp.float32
    dma = pltpu.SemaphoreType.DMA
    notes = [pltpu.VMEM((8, devices), i32), pltpu.SMEM((8, devices), i32)]
    by_part = (1, 0, 2)
    pos = positions.transpose(by_part)
    stay = lambda x: pltpu.with_memory_space_constraint(x, pltpu.HBM)
    others = lax.ppermute(winds, "lat", [(i, i ^ 1) for i in range(lax.axis_size("lat"))])
    both = jnp.stack([winds, others]).reshape(2 * MB, 3 * LEV, MBC)
    box, places = pl.pallas_call(
        pack_kernel,
        name="pack",
        out_shape=(
            jax.ShapeDtypeStruct((devices * ROWS, BLK), i32),
            jax.ShapeDtypeStruct((8, blocks), i32),
        ),
        in_specs=[hbm] * 6,
        out_specs=(vmem, smem),
        scratch_shapes=[
            pltpu.VMEM((1, blocks), i32),
            pltpu.VMEM((Q, devices), i32),
            pltpu.VMEM((1, blocks), i32),
            pltpu.VMEM((blocks, BLK), i32),
            pltpu.VMEM((3, blocks, BLK), f32),
            pltpu.VMEM((blocks, S, BLK), f32),
            pltpu.VMEM((2 * blocks, BLK), i32),
            pltpu.VMEM((8, blocks), i32),
            dma((7,)),
        ],
        compiler_params=params,
    )(
        stay(block_slots.transpose(1, 0)),
        stay(requests.reshape(devices, Q).transpose(1, 0)),
        stay(destinations.transpose(1, 0)),
        stay(cell_keys),
        stay(pos),
        stay(mass),
    )
    box = swap(box, devices)
    local_wind = pl.pallas_call(
        sample_kernel,
        name="sample",
        out_shape=jax.ShapeDtypeStruct((devices * WIND_ROWS, BLK), i32),
        in_specs=[vmem] * 2,
        out_specs=vmem,
        scratch_shapes=[
            pltpu.SMEM((devices * ROOM + ROOM,), i32),
            pltpu.VMEM((devices * 2 * ROOM, BLK), i32),
            *notes,
            dma,
        ],
        compiler_params=params,
    )(box, both)
    room = devices * CAP + MB + 2 * PAIR_UNROLL
    assert room + devices * CAP <= HOMES_AT and HOMES_AT + (room + devices * CAP) // 2 < PAIRS_AT
    plan, shares = pl.pallas_call(
        order_kernel,
        name="order",
        cost_estimate=pl.CostEstimate(flops=10**9, bytes_accessed=20 << 20, transcendentals=0),
        out_shape=(
            jax.ShapeDtypeStruct((PLAN,), i32),
            jax.ShapeDtypeStruct((room * S, BLK), f32),
        ),
        in_specs=[vmem],
        out_specs=(smem, vmem),
        scratch_shapes=[
            *notes,
            pltpu.SMEM((MB + 1,), i32),
            pltpu.SMEM((MB + 1,), i32),
            dma,
        ],
        compiler_params=params,
    )(box)
    returned = swap(local_wind, devices)
    drift = (pos, velocity.transpose(by_part), increments.transpose(by_part))
    row_scratch = pltpu.VMEM((blocks, BLK), i32)
    outbox = pl.pallas_call(
        height_kernel,
        name="height",
        out_shape=jax.ShapeDtypeStruct((devices * CAP, BLK), i32),
        in_specs=[smem, whole(pl.ANY)] + [vmem] * 5,
        out_specs=vmem,
        scratch_shapes=[row_scratch],
        compiler_params=params,
    )(
        places,
        plan,
        returned,
        *drift,
        cell_keys,
    )
    inbox = swap(outbox, devices)
    moved, turbulence = pl.pallas_call(
        move_kernel,
        name="move",
        out_shape=[jax.ShapeDtypeStruct(pos.shape, f32)] * 2,
        in_specs=[smem] + [vmem] * 4,
        out_specs=[vmem] * 2,
        scratch_shapes=[row_scratch, row_scratch],
        cost_estimate=pl.CostEstimate(flops=10**7, bytes_accessed=2 << 20, transcendentals=0),
        compiler_params=params,
    )(places, returned, *drift)
    total = pl.pallas_call(
        deposit_kernel,
        name="deposit",
        out_shape=jax.ShapeDtypeStruct((MB, S * LEV, MBC), f32),
        in_specs=[smem, vmem, vmem],
        out_specs=hbm,
        scratch_shapes=[pltpu.VMEM((MB, S * LEV, MBC), f32), dma((MB,))],
        compiler_params=params,
    )(plan, inbox, shares)
    return (
        moved.transpose(by_part),
        turbulence.transpose(by_part),
        total.reshape(winds.shape[:2] + (S, LEV, MBC)),
    )


def solution(mesh):
    rows = P(AXES, None, None)
    pairs = P(AXES, None)
    tiles = P("lat", "lon", None, None, None)
    return jax.shard_map(
        body,
        mesh=mesh,
        in_specs=(tiles, rows, rows, rows, rows, rows, pairs, pairs, pairs),
        out_specs=(rows, rows, tiles),
        check_vma=False,
    )
```

```python
import jax
import jax.numpy as jnp
from jax import lax
from jax.experimental import pallas as pl
from jax.experimental.pallas import tpu as pltpu
from jax.sharding import PartitionSpec as P

BY = 8
BX = 16
MBC = 128
LEV = 40
S = 8
BLK = 128
MB = 16
Q = 2
CAP = 2
ROOM = Q * CAP

DECAY = 0.8
KICK = 0.6
STEP = 0.5

AXES = ("lat", "lon")
LOW16 = 0xFFFF
ROW_SCALE = 65535.0 / (BY - 1)
COL_SCALE = 65535.0 / (BX - 1)
LEV_SCALE = 65535.0 / (LEV - 1)
Z_SCALE = float((1 << 20) - 1) / (LEV - 1)
W_TOP = 6.1
W_SCALE = 65535.0 / (2 * W_TOP)
M_SCALE = 32767.0
SAMPLE_UNROLL = 12
PAIR_UNROLL = 16
PAIR_TAIL = 4

HIGH_ROW = ROOM
NOTE_ROW = HIGH_ROW + ROOM // 2
SHARE_ROW = NOTE_ROW + 1
ROWS = SHARE_ROW + CAP * S // 2
WIND_ROWS = ROOM + ROOM // 2
HOME_AT = ROOM
LANDED_AT = HOME_AT + CAP
TAKEN_AT = LANDED_AT + 1
EACH = 8
PLAN = 1024
HOMES_AT = 576
PAIRS_AT = PLAN - 1


def hat(offset):
    return jnp.maximum(0.0, 1.0 - jnp.abs(offset))


def fixed(value, scale, shift=0.0):
    return ((value + shift) * scale + 0.5).astype(jnp.int32)


def upper(word):
    return lax.shift_right_logical(word, jnp.int32(16)).astype(jnp.float32)


def lower(word):
    return (word & LOW16).astype(jnp.float32)


def whole(space=pltpu.VMEM):
    return pl.BlockSpec(memory_space=space)


def read_notes(box, rows, notes, sem):
    devices = notes.shape[1]
    sent = upper(box[pl.ds(NOTE_ROW, devices, stride=ROWS), :])
    rows[...] = sent.T[0 : notes.shape[0], :].astype(jnp.int32)
    copy = pltpu.make_async_copy(rows, notes, sem)
    copy.start()
    copy.wait()


def pack_kernel(
    slots_hbm, asked_hbm, targets_hbm, keys_hbm, pos_hbm, mass_hbm,
    box, places,
    slots, asked, targets, keys, pos, mass, yx_rows, z_rows, heights, ranks, sems,
):
    blocks, devices = mass.shape[0], asked.shape[1]
    copies = [
        pltpu.make_async_copy(src, dst, sems.at[i])
        for i, (src, dst) in enumerate(
            (
                (slots_hbm, slots),
                (targets_hbm, targets),
                (asked_hbm, asked),
                (keys_hbm, keys),
                (pos_hbm, pos),
                (mass_hbm, mass),
            )
        )
    ]
    for copy in copies:
        copy.start()
    square = (blocks, blocks)
    down = lax.broadcasted_iota(jnp.int32, square, 0)
    along = lax.broadcasted_iota(jnp.int32, square, 1)

    def stand(row):
        return jnp.broadcast_to(row.astype(jnp.float32), square).T.astype(jnp.int32)

    def rank(row):
        same = (stand(row) == row) & (down < along)
        return jnp.sum(jnp.where(same, 1.0, 0.0), axis=0, keepdims=True).astype(jnp.int32)

    copies[0].wait()
    slot = slots[...]
    tile = slot >> 1
    order = rank(tile)
    lons = lax.axis_size("lon")
    core = (tile >> (lons.bit_length() - 1)) & 1
    helper = (order + lax.axis_index("lat") + lax.axis_index("lon")) & 1
    host = tile + (helper - core) * lons
    seat = core * (ROOM // 2) + (order >> 1)
    copies[1].wait()
    target = targets[...]
    turn = rank(target)
    ranks[0:1, :] = host * ROWS + seat
    ranks[1:2, :] = target * ROWS + SHARE_ROW + turn * (S // 2)
    ranks[2:3, :] = host * WIND_ROWS + seat
    ranks[3:4, :] = host * WIND_ROWS + ROOM + (seat >> 1)
    ranks[4:5, :] = 16 - 16 * (seat & 1)
    ranks[5:6, :] = target * CAP + turn
    ranks[6:7, :] = host * ROOM + seat
    ranked = pltpu.make_async_copy(ranks, places, sems.at[len(copies)])
    ranked.start()
    bits = stand((turn << 15) | (seat << 13) | (helper << 12) | slot)
    slot_down = bits & 0xFFF
    helper_down = (bits >> 12) & 1
    seat_down = (bits >> 13) & (ROOM - 1)
    turn_down = bits >> 15
    core_down = seat_down >> 1
    copies[2].wait()
    met = jnp.where((slot_down & 1) == 0, asked[0:1, :], asked[1:2, :])
    met = jnp.where((slot_down >> 1) == along, met, 0).astype(jnp.float32)
    met = jnp.sum(met, axis=1, keepdims=True)
    met = met + jnp.where(helper_down == core_down, 0.0, float(MB))
    copies[3].wait()
    home = (keys[:, 0:1] >> 7).astype(jnp.float32)
    said = jnp.where(along == seat_down, met, 0.0)
    said = jnp.where(along == TAKEN_AT, jnp.where(core_down == 0, 1.0, float(EACH)), said)
    more = jnp.where(along == HOME_AT + turn_down, home, 0.0) + jnp.where(
        along == LANDED_AT, 1.0, 0.0
    )
    mine = jnp.concatenate([down == host, down == target], axis=1)
    notes = jnp.dot(
        jnp.where(mine, 1.0, 0.0).astype(jnp.bfloat16),
        jnp.concatenate([said, more], axis=0).astype(jnp.bfloat16),
        preferred_element_type=jnp.float32,
    )
    copies[4].wait()
    yx_rows[...] = (fixed(pos[0], ROW_SCALE) << 16) | fixed(pos[1], COL_SCALE)
    z_rows[...] = fixed(pos[2], Z_SCALE)
    copies[5].wait()
    ranked.wait()

    def put(b, _):
        box[pl.ds(places[0, b], 1), :] = yx_rows[pl.ds(b, 1), :]
        heights[pl.ds(places[6, b], 1), :] = z_rows[pl.ds(b, 1), :]
        share = fixed(mass[b], M_SCALE)
        box[pl.ds(places[1, b], S // 2), :] = (share[0 : S // 2] << 16) | share[S // 2 :]
        return 0

    lax.fori_loop(0, blocks, put, 0, unroll=16)
    each = [heights[pl.ds(k, devices, stride=ROOM), :] for k in range(ROOM)]
    for k in range(0, ROOM, 2):
        box[pl.ds(HIGH_ROW + k // 2, devices, stride=ROWS), :] = ((each[k] >> 4) << 16) | (
            (each[k + 1] >> 4) & LOW16
        )
    word = notes.astype(jnp.int32) << 16
    for k in range(ROOM):
        word = word | ((each[k] & 15) << (12 - 4 * k))
    box[pl.ds(NOTE_ROW, devices, stride=ROWS), :] = word


def sample_kernel(box, winds, out, queue, found, rows, notes, sem):
    devices = notes.shape[1]
    read_notes(box, rows, notes, sem)

    def enlist(t, n):
        taken = notes[TAKEN_AT, t]
        for r in range(ROOM // 2):
            queue[n + r] = t * ROOM + r
        n = n + (taken & (EACH - 1))
        for r in range(ROOM // 2):
            queue[n + r] = t * ROOM + ROOM // 2 + r
        return n + (taken >> 3)

    n = lax.fori_loop(0, devices, enlist, 0, unroll=4)
    levels = lax.broadcasted_iota(jnp.int32, (LEV, BLK), 0).astype(jnp.float32)
    lats = lax.broadcasted_iota(jnp.int32, (BY, BLK), 0).astype(jnp.float32)
    lons = lax.broadcasted_iota(jnp.int32, (BX, BLK), 0).astype(jnp.float32)

    def step(i, _):
        for j in range(SAMPLE_UNROLL):
            item = queue[jnp.minimum(i * SAMPLE_UNROLL + j, n - 1)]
            src, seat = item >> 2, item & (ROOM - 1)
            row = src * ROWS
            yx = box[pl.ds(row + seat, 1), :]
            high = lax.shift_right_logical(
                box[pl.ds(row + HIGH_ROW + (seat >> 1), 1), :],
                jnp.full((1, BLK), 16 - 16 * (seat & 1), jnp.int32),
            )
            low = box[pl.ds(row + NOTE_ROW, 1), :] >> jnp.full((1, BLK), 12 - 4 * seat, jnp.int32)
            height = ((high & LOW16) << 4) | (low & 15)
            hy = hat(upper(yx) * (1.0 / ROW_SCALE) - lats)
            hx = hat(lower(yx) * (1.0 / COL_SCALE) - lons)
            wz = hat(height.astype(jnp.float32) * (1.0 / Z_SCALE) - levels)
            wz = wz.astype(jnp.bfloat16).astype(jnp.float32)
            flat = (hy[:, None, :] * hx[None, :, :]).reshape(MBC, BLK)
            high = flat.astype(jnp.bfloat16)
            low = (flat - high.astype(jnp.float32)).astype(jnp.bfloat16)
            met = winds[notes[seat, src]]
            level_wind = jnp.dot(met, high, preferred_element_type=jnp.float32) + jnp.dot(
                met, low, preferred_element_type=jnp.float32
            )
            wind = [
                jnp.sum(level_wind[c * LEV : (c + 1) * LEV] * wz, axis=0, keepdims=True)
                for c in range(3)
            ]
            found[pl.ds(2 * item, 1), :] = (fixed(wind[0], W_SCALE, W_TOP) << 16) | fixed(
                wind[1], W_SCALE, W_TOP
            )
            found[pl.ds(2 * item + 1, 1), :] = fixed(wind[2], W_SCALE, W_TOP)
        return 0

    lax.fori_loop(0, pl.cdiv(n, SAMPLE_UNROLL), step, 0)

    def every(r):
        return found[pl.ds(r, devices, stride=2 * ROOM), :]

    for r in range(ROOM):
        out[pl.ds(r, devices, stride=WIND_ROWS), :] = every(2 * r)
    for r in range(0, ROOM, 2):
        out[pl.ds(ROOM + r // 2, devices, stride=WIND_ROWS), :] = (every(2 * r + 1) << 16) | (
            every(2 * r + 3) & LOW16
        )


def order_kernel(box, plan, shares, rows, notes, starts, tally, sem):
    devices = notes.shape[1]
    read_notes(box, rows, notes, sem)

    room = shares.shape[0] // S

    def clear(i, _):
        plan[i] = -1
        return 0

    lax.fori_loop(0, room, clear, 0, unroll=8)

    def clear_home(i, _):
        plan[HOMES_AT + i] = 0
        return 0

    lax.fori_loop(0, room // 2, clear_home, 0, unroll=8)
    for h in range(MB):
        tally[h] = 0

    def tell(t, _):
        landed = notes[LANDED_AT, t]
        for r in range(CAP):
            home = jnp.where(r < landed, notes[HOME_AT + r, t], MB)
            tally[home] = tally[home] + 1
        return 0

    tally[MB] = 0
    lax.fori_loop(0, devices, tell, 0, unroll=4)
    n = jnp.int32(0)
    for h in range(MB):
        starts[h] = n
        n = n + ((tally[h] + 1) & ~1)
    starts[MB] = room

    def place(t, _):
        landed = notes[LANDED_AT, t]
        for r in range(CAP):
            there = r < landed
            home = jnp.where(there, notes[HOME_AT + r, t], MB)
            at = starts[home]
            starts[home] = at + 1
            plan[at] = jnp.where(there, t * CAP + r, -1)
            plan[HOMES_AT + (at >> 1)] = jnp.where(there, home, 0)
        return 0

    lax.fori_loop(0, devices, place, 0, unroll=4)
    plan[PAIRS_AT] = n >> 1

    def expand(i, _):
        for j in range(2 * PAIR_UNROLL):
            at = i * 2 * PAIR_UNROLL + j
            item = plan[at]
            row = jnp.maximum(item, 0)
            packed = box[pl.ds((row >> 1) * ROWS + SHARE_ROW + (row & 1) * (S // 2), S // 2), :]
            unit = jnp.where(item < 0, 0.0, 1.0 / M_SCALE)
            shares[pl.ds(S * at, S), :] = (
                jnp.concatenate([upper(packed), lower(packed)], axis=0) * unit
            )
        return 0

    lax.fori_loop(0, jnp.maximum(pl.cdiv(n, 2 * PAIR_UNROLL), 1), expand, 0)


def advance(pos, vel, noise, word, top):
    wind = word * (1.0 / W_SCALE) - W_TOP
    fresh = DECAY * vel + KICK * noise
    return fresh, jnp.clip(pos + STEP * (wind + fresh), 0.0, top)


def take_up(places, box, z_rows):
    def take(b, _):
        z_rows[pl.ds(b, 1), :] = lax.shift_right_logical(
            box[pl.ds(places[3, b], 1), :], jnp.full((1, BLK), places[4, b], jnp.int32)
        )
        return 0

    lax.fori_loop(0, z_rows.shape[0], take, 0, unroll=8)
    return lower(z_rows[...])


def height_kernel(places, plan, box, pos, vel, noise, keys, out):
    def put(b, _):
        row = pl.ds(b, 1)
        word = lax.shift_right_logical(
            box[pl.ds(places[3, b], 1), :], jnp.full((1, BLK), places[4, b], jnp.int32)
        )
        _, height = advance(pos[2, row], vel[2, row], noise[2, row], lower(word), LEV - 1.0)
        out[pl.ds(places[5, b], 1), :] = (keys[row, :] << 16) | fixed(height, LEV_SCALE)
        return 0

    lax.fori_loop(0, keys.shape[0], put, 0, unroll=16)


def move_kernel(places, box, pos, vel, noise, moved, turb, yx_rows, z_rows):
    def take(b, _):
        yx_rows[pl.ds(b, 1), :] = box[pl.ds(places[2, b], 1), :]
        return 0

    lax.fori_loop(0, yx_rows.shape[0], take, 0, unroll=8)
    yx = yx_rows[...]
    words = (upper(yx), lower(yx), take_up(places, box, z_rows))
    for c, top in enumerate((BY - 1.0, BX - 1.0, LEV - 1.0)):
        turb[c], moved[c] = advance(pos[c], vel[c], noise[c], words[c], top)


def deposit_kernel(plan, box, shares, out, total, sems):
    n = plan[PAIRS_AT]
    total[...] = jnp.zeros(total.shape, jnp.float32)
    level = lax.broadcasted_iota(jnp.int32, (8, BLK), 0).astype(jnp.float32)
    cells = lax.broadcasted_iota(jnp.int32, (MBC, BLK), 0).astype(jnp.float32)
    cells = cells.astype(jnp.bfloat16)
    one, none = jnp.bfloat16(1), jnp.bfloat16(0)

    def step(first, length, done):
        for j in range(length):
            pair = first + j
            weights, picks = [], []
            for half in range(2):
                at = 2 * pair + half
                row = jnp.maximum(plan[at], 0)
                word = box[pl.ds(row, 1), :]
                height = jnp.broadcast_to(lower(word) * (1.0 / LEV_SCALE), (8, BLK))
                vert = [hat(height - (level + 8.0 * k)) for k in range(LEV // 8)]
                held = [
                    shares[pl.ds(S * at + s, 8, stride=0), :] * part for s in range(S) for part in vert
                ]
                weights.append(jnp.concatenate(held, axis=0).astype(jnp.bfloat16))
                cell = (word >> 16) & (MBC - 1)
                cell = cell.astype(jnp.float32).astype(jnp.bfloat16)
                picks.append(jnp.where(cells == cell, one, none))
            part = lax.dot_general(
                jnp.concatenate(weights, axis=1),
                jnp.concatenate(picks, axis=1),
                (((1,), (1,)), ((), ())),
                preferred_element_type=jnp.float32,
            )
            home = plan[HOMES_AT + pair]
            total[home] = total[home] + part
        later = first + length
        final = jnp.where(later < n, plan[HOMES_AT + later], MB)

        def leave(h, _):
            pltpu.make_async_copy(total.at[h], out.at[h], sems.at[h]).start()
            return 0

        lax.fori_loop(done, final, leave, 0)
        return final

    steps = (n + PAIR_UNROLL // 2 - 1) // PAIR_UNROLL
    done = lax.fori_loop(
        0, steps, lambda i, done: step(i * PAIR_UNROLL, PAIR_UNROLL, done), jnp.int32(0)
    )
    start = steps * PAIR_UNROLL
    short = jnp.maximum(pl.cdiv(n - start, PAIR_TAIL), jnp.where(steps == 0, 1, 0))
    lax.fori_loop(0, short, lambda i, done: step(start + i * PAIR_TAIL, PAIR_TAIL, done), done)
    for h in range(MB):
        pltpu.make_async_copy(total.at[h], out.at[h], sems.at[h]).wait()


def swap(box, devices):
    rows = box.shape[0] // devices
    step = 8 if rows % 8 == 0 else 2 if rows % 2 == 0 else 1
    whole_box = box.reshape(devices * rows // step, step, BLK)
    arrived = lax.all_to_all(whole_box, AXES, split_axis=0, concat_axis=0, tiled=True)
    return arrived.reshape(box.shape)


def body(
    winds, positions, velocity, increments, mass, requests, block_slots, destinations, cell_keys
):
    devices = lax.axis_size("lat") * lax.axis_size("lon")
    blocks = positions.shape[0]
    params = pltpu.CompilerParams(vmem_limit_bytes=40 << 20)
    smem, vmem, hbm = whole(pltpu.SMEM), whole(), whole(pltpu.HBM)
    i32, f32 = jnp.int32, jnp.float32
    dma = pltpu.SemaphoreType.DMA
    notes = [pltpu.VMEM((8, devices), i32), pltpu.SMEM((8, devices), i32)]
    by_part = (1, 0, 2)
    pos = positions.transpose(by_part)
    stay = lambda x: pltpu.with_memory_space_constraint(x, pltpu.HBM)
    others = lax.ppermute(winds, "lat", [(i, i ^ 1) for i in range(lax.axis_size("lat"))])
    both = jnp.stack([winds, others]).reshape(2 * MB, 3 * LEV, MBC)
    box, places = pl.pallas_call(
        pack_kernel,
        name="pack",
        out_shape=(
            jax.ShapeDtypeStruct((devices * ROWS, BLK), i32),
            jax.ShapeDtypeStruct((8, blocks), i32),
        ),
        in_specs=[hbm] * 6,
        out_specs=(vmem, smem),
        scratch_shapes=[
            pltpu.VMEM((1, blocks), i32),
            pltpu.VMEM((Q, devices), i32),
            pltpu.VMEM((1, blocks), i32),
            pltpu.VMEM((blocks, BLK), i32),
            pltpu.VMEM((3, blocks, BLK), f32),
            pltpu.VMEM((blocks, S, BLK), f32),
            pltpu.VMEM((blocks, BLK), i32),
            pltpu.VMEM((blocks, BLK), i32),
            pltpu.VMEM((devices * ROOM, BLK), i32),
            pltpu.VMEM((8, blocks), i32),
            dma((7,)),
        ],
        compiler_params=params,
    )(
        stay(block_slots.transpose(1, 0)),
        stay(requests.reshape(devices, Q).transpose(1, 0)),
        stay(destinations.transpose(1, 0)),
        stay(cell_keys),
        stay(pos),
        stay(mass),
    )
    box = swap(box, devices)
    local_wind = pl.pallas_call(
        sample_kernel,
        name="sample",
        out_shape=jax.ShapeDtypeStruct((devices * WIND_ROWS, BLK), i32),
        in_specs=[vmem] * 2,
        out_specs=vmem,
        scratch_shapes=[
            pltpu.SMEM((devices * ROOM + ROOM,), i32),
            pltpu.VMEM((devices * 2 * ROOM, BLK), i32),
            *notes,
            dma,
        ],
        compiler_params=params,
    )(box, both)
    room = devices * CAP + MB + 2 * PAIR_UNROLL
    assert room + devices * CAP <= HOMES_AT and HOMES_AT + (room + devices * CAP) // 2 < PAIRS_AT
    plan, shares = pl.pallas_call(
        order_kernel,
        name="order",
        cost_estimate=pl.CostEstimate(flops=10**9, bytes_accessed=20 << 20, transcendentals=0),
        out_shape=(
            jax.ShapeDtypeStruct((PLAN,), i32),
            jax.ShapeDtypeStruct((room * S, BLK), f32),
        ),
        in_specs=[vmem],
        out_specs=(smem, vmem),
        scratch_shapes=[
            *notes,
            pltpu.SMEM((MB + 1,), i32),
            pltpu.SMEM((MB + 1,), i32),
            dma,
        ],
        compiler_params=params,
    )(box)
    returned = swap(local_wind, devices)
    drift = (pos, velocity.transpose(by_part), increments.transpose(by_part))
    row_scratch = pltpu.VMEM((blocks, BLK), i32)
    outbox = pl.pallas_call(
        height_kernel,
        name="height",
        out_shape=jax.ShapeDtypeStruct((devices * CAP, BLK), i32),
        in_specs=[smem, whole(pl.ANY)] + [vmem] * 5,
        out_specs=vmem,
        compiler_params=params,
    )(
        places,
        plan,
        returned,
        *drift,
        cell_keys,
    )
    inbox = swap(outbox, devices)
    moved, turbulence = pl.pallas_call(
        move_kernel,
        name="move",
        out_shape=[jax.ShapeDtypeStruct(pos.shape, f32)] * 2,
        in_specs=[smem] + [vmem] * 4,
        out_specs=[vmem] * 2,
        scratch_shapes=[row_scratch, row_scratch],
        cost_estimate=pl.CostEstimate(flops=10**7, bytes_accessed=2 << 20, transcendentals=0),
        compiler_params=params,
    )(places, returned, *drift)
    total = pl.pallas_call(
        deposit_kernel,
        name="deposit",
        out_shape=jax.ShapeDtypeStruct((MB, S * LEV, MBC), f32),
        in_specs=[smem, vmem, vmem],
        out_specs=hbm,
        scratch_shapes=[pltpu.VMEM((MB, S * LEV, MBC), f32), dma((MB,))],
        compiler_params=params,
    )(plan, inbox, shares)
    return (
        moved.transpose(by_part),
        turbulence.transpose(by_part),
        total.reshape(winds.shape[:2] + (S, LEV, MBC)),
    )


def solution(mesh):
    rows = P(AXES, None, None)
    pairs = P(AXES, None)
    tiles = P("lat", "lon", None, None, None)
    return jax.shard_map(
        body,
        mesh=mesh,
        in_specs=(tiles, rows, rows, rows, rows, rows, pairs, pairs, pairs),
        out_specs=(rows, rows, tiles),
        check_vma=False,
    )
```

```python
import jax
import jax.numpy as jnp
from jax import lax
from jax.experimental import pallas as pl
from jax.experimental.pallas import tpu as pltpu
from jax.sharding import PartitionSpec as P

BY = 8
BX = 16
MBC = 128
LEV = 40
S = 8
BLK = 128
MB = 16
Q = 2
CAP = 2
ROOM = Q * CAP

DECAY = 0.8
KICK = 0.6
STEP = 0.5

AXES = ("lat", "lon")
LOW16 = 0xFFFF
ROW_SCALE = 65535.0 / (BY - 1)
COL_SCALE = 65535.0 / (BX - 1)
LEV_SCALE = 65535.0 / (LEV - 1)
Z_SCALE = float((1 << 20) - 1) / (LEV - 1)
W_TOP = 6.1
W_SCALE = 65535.0 / (2 * W_TOP)
M_SCALE = 32767.0
SAMPLE_UNROLL = 14
PAIR_UNROLL = 16
PAIR_TAIL = 4

HIGH_ROW = ROOM
NOTE_ROW = HIGH_ROW + ROOM // 2
SHARE_ROW = NOTE_ROW + 1
ROWS = SHARE_ROW + CAP * S // 2
WIND_ROWS = ROOM + ROOM // 2
HOME_AT = ROOM
LANDED_AT = HOME_AT + CAP
TAKEN_AT = LANDED_AT + 1
EACH = 8
PLAN = 1024
HOMES_AT = 576
PAIRS_AT = PLAN - 1


def hat(offset):
    return jnp.maximum(0.0, 1.0 - jnp.abs(offset))


def fixed(value, scale, shift=0.0):
    return ((value + shift) * scale + 0.5).astype(jnp.int32)


def upper(word):
    return lax.shift_right_logical(word, jnp.int32(16)).astype(jnp.float32)


def lower(word):
    return (word & LOW16).astype(jnp.float32)


def whole(space=pltpu.VMEM):
    return pl.BlockSpec(memory_space=space)


def read_notes(box, rows, notes, sem):
    devices = notes.shape[1]
    sent = upper(box[pl.ds(NOTE_ROW, devices, stride=ROWS), :])
    rows[...] = sent.T[0 : notes.shape[0], :].astype(jnp.int32)
    copy = pltpu.make_async_copy(rows, notes, sem)
    copy.start()
    copy.wait()


def pack_kernel(
    slots_hbm, asked_hbm, targets_hbm, keys_hbm, pos_hbm, mass_hbm,
    box, places,
    slots, asked, targets, keys, pos, mass, yx_rows, z_rows, heights, ranks, sems,
):
    blocks, devices = mass.shape[0], asked.shape[1]
    copies = [
        pltpu.make_async_copy(src, dst, sems.at[i])
        for i, (src, dst) in enumerate(
            (
                (slots_hbm, slots),
                (targets_hbm, targets),
                (asked_hbm, asked),
                (keys_hbm, keys),
                (pos_hbm, pos),
                (mass_hbm, mass),
            )
        )
    ]
    for copy in copies:
        copy.start()
    square = (blocks, blocks)
    down = lax.broadcasted_iota(jnp.int32, square, 0)
    along = lax.broadcasted_iota(jnp.int32, square, 1)

    def stand(row):
        return jnp.broadcast_to(row.astype(jnp.float32), square).T.astype(jnp.int32)

    def rank(row):
        same = (stand(row) == row) & (down < along)
        return jnp.sum(jnp.where(same, 1.0, 0.0), axis=0, keepdims=True).astype(jnp.int32)

    copies[0].wait()
    slot = slots[...]
    tile = slot >> 1
    order = rank(tile)
    lons = lax.axis_size("lon")
    core = (tile >> (lons.bit_length() - 1)) & 1
    helper = (order + lax.axis_index("lat") + lax.axis_index("lon")) & 1
    host = tile + (helper - core) * lons
    seat = core * (ROOM // 2) + (order >> 1)
    copies[1].wait()
    target = targets[...]
    turn = rank(target)
    ranks[0:1, :] = host * ROWS + seat
    ranks[1:2, :] = target * ROWS + SHARE_ROW + turn * (S // 2)
    ranks[2:3, :] = host * WIND_ROWS + seat
    ranks[3:4, :] = host * WIND_ROWS + ROOM + (seat >> 1)
    ranks[4:5, :] = 16 - 16 * (seat & 1)
    ranks[5:6, :] = target * CAP + turn
    ranks[6:7, :] = host * ROOM + seat
    ranked = pltpu.make_async_copy(ranks, places, sems.at[len(copies)])
    ranked.start()
    bits = stand((turn << 15) | (seat << 13) | (helper << 12) | slot)
    slot_down = bits & 0xFFF
    helper_down = (bits >> 12) & 1
    seat_down = (bits >> 13) & (ROOM - 1)
    turn_down = bits >> 15
    core_down = seat_down >> 1
    copies[2].wait()
    met = jnp.where((slot_down & 1) == 0, asked[0:1, :], asked[1:2, :])
    met = jnp.where((slot_down >> 1) == along, met, 0).astype(jnp.float32)
    met = jnp.sum(met, axis=1, keepdims=True)
    met = met + jnp.where(helper_down == core_down, 0.0, float(MB))
    copies[3].wait()
    home = (keys[:, 0:1] >> 7).astype(jnp.float32)
    said = jnp.where(along == seat_down, met, 0.0)
    said = jnp.where(along == TAKEN_AT, jnp.where(core_down == 0, 1.0, float(EACH)), said)
    more = jnp.where(along == HOME_AT + turn_down, home, 0.0) + jnp.where(
        along == LANDED_AT, 1.0, 0.0
    )
    mine = jnp.concatenate([down == host, down == target], axis=1)
    notes = jnp.dot(
        jnp.where(mine, 1.0, 0.0).astype(jnp.bfloat16),
        jnp.concatenate([said, more], axis=0).astype(jnp.bfloat16),
        preferred_element_type=jnp.float32,
    )
    copies[4].wait()
    yx_rows[...] = (fixed(pos[0], ROW_SCALE) << 16) | fixed(pos[1], COL_SCALE)
    z_rows[...] = fixed(pos[2], Z_SCALE)
    copies[5].wait()
    ranked.wait()

    def put(b, _):
        box[pl.ds(places[0, b], 1), :] = yx_rows[pl.ds(b, 1), :]
        heights[pl.ds(places[6, b], 1), :] = z_rows[pl.ds(b, 1), :]
        share = fixed(mass[b], M_SCALE)
        box[pl.ds(places[1, b], S // 2), :] = (share[0 : S // 2] << 16) | share[S // 2 :]
        return 0

    lax.fori_loop(0, blocks, put, 0, unroll=16)
    each = [heights[pl.ds(k, devices, stride=ROOM), :] for k in range(ROOM)]
    for k in range(0, ROOM, 2):
        box[pl.ds(HIGH_ROW + k // 2, devices, stride=ROWS), :] = ((each[k] >> 4) << 16) | (
            (each[k + 1] >> 4) & LOW16
        )
    word = notes.astype(jnp.int32) << 16
    for k in range(ROOM):
        word = word | ((each[k] & 15) << (12 - 4 * k))
    box[pl.ds(NOTE_ROW, devices, stride=ROWS), :] = word


def sample_kernel(box, winds, out, queue, found, rows, notes, sem):
    devices = notes.shape[1]
    read_notes(box, rows, notes, sem)

    def enlist(t, n):
        taken = notes[TAKEN_AT, t]
        for r in range(ROOM // 2):
            queue[n + r] = t * ROOM + r
        n = n + (taken & (EACH - 1))
        for r in range(ROOM // 2):
            queue[n + r] = t * ROOM + ROOM // 2 + r
        return n + (taken >> 3)

    n = lax.fori_loop(0, devices, enlist, 0, unroll=16)
    levels = lax.broadcasted_iota(jnp.int32, (LEV, BLK), 0).astype(jnp.float32)
    lats = lax.broadcasted_iota(jnp.int32, (BY, BLK), 0).astype(jnp.float32)
    lons = lax.broadcasted_iota(jnp.int32, (BX, BLK), 0).astype(jnp.float32)

    def step(i, _):
        for j in range(SAMPLE_UNROLL):
            item = queue[jnp.minimum(i * SAMPLE_UNROLL + j, n - 1)]
            src, seat = item >> 2, item & (ROOM - 1)
            row = src * ROWS
            yx = box[pl.ds(row + seat, 1), :]
            high = lax.shift_right_logical(
                box[pl.ds(row + HIGH_ROW + (seat >> 1), 1), :],
                jnp.full((1, BLK), 16 - 16 * (seat & 1), jnp.int32),
            )
            low = box[pl.ds(row + NOTE_ROW, 1), :] >> jnp.full((1, BLK), 12 - 4 * seat, jnp.int32)
            height = ((high & LOW16) << 4) | (low & 15)
            hy = hat(upper(yx) * (1.0 / ROW_SCALE) - lats)
            hx = hat(lower(yx) * (1.0 / COL_SCALE) - lons)
            wz = hat(height.astype(jnp.float32) * (1.0 / Z_SCALE) - levels)
            wz = wz.astype(jnp.bfloat16).astype(jnp.float32)
            flat = (hy[:, None, :] * hx[None, :, :]).reshape(MBC, BLK)
            high = flat.astype(jnp.bfloat16)
            low = (flat - high.astype(jnp.float32)).astype(jnp.bfloat16)
            met = winds[notes[seat, src]]
            level_wind = jnp.dot(met, high, preferred_element_type=jnp.float32) + jnp.dot(
                met, low, preferred_element_type=jnp.float32
            )
            wind = [
                jnp.sum(level_wind[c * LEV : (c + 1) * LEV] * wz, axis=0, keepdims=True)
                for c in range(3)
            ]
            found[pl.ds(2 * item, 1), :] = (fixed(wind[0], W_SCALE, W_TOP) << 16) | fixed(
                wind[1], W_SCALE, W_TOP
            )
            found[pl.ds(2 * item + 1, 1), :] = fixed(wind[2], W_SCALE, W_TOP)
        return 0

    lax.fori_loop(0, pl.cdiv(n, SAMPLE_UNROLL), step, 0)

    def every(r):
        return found[pl.ds(r, devices, stride=2 * ROOM), :]

    for r in range(ROOM):
        out[pl.ds(r, devices, stride=WIND_ROWS), :] = every(2 * r)
    for r in range(0, ROOM, 2):
        out[pl.ds(ROOM + r // 2, devices, stride=WIND_ROWS), :] = (every(2 * r + 1) << 16) | (
            every(2 * r + 3) & LOW16
        )


def order_kernel(box, plan, shares, rows, notes, starts, tally, sem):
    devices = notes.shape[1]
    read_notes(box, rows, notes, sem)

    room = shares.shape[0] // S

    def clear(i, _):
        plan[i] = -1
        return 0

    lax.fori_loop(0, room, clear, 0, unroll=8)

    def clear_home(i, _):
        plan[HOMES_AT + i] = 0
        return 0

    lax.fori_loop(0, room // 2, clear_home, 0, unroll=8)
    for h in range(MB):
        tally[h] = 0

    def tell(t, _):
        landed = notes[LANDED_AT, t]
        for r in range(CAP):
            home = jnp.where(r < landed, notes[HOME_AT + r, t], MB)
            tally[home] = tally[home] + 1
        return 0

    tally[MB] = 0
    lax.fori_loop(0, devices, tell, 0, unroll=4)
    n = jnp.int32(0)
    for h in range(MB):
        starts[h] = n
        n = n + ((tally[h] + 1) & ~1)
    starts[MB] = room

    def place(t, _):
        landed = notes[LANDED_AT, t]
        for r in range(CAP):
            there = r < landed
            home = jnp.where(there, notes[HOME_AT + r, t], MB)
            at = starts[home]
            starts[home] = at + 1
            plan[at] = jnp.where(there, t * CAP + r, -1)
            plan[HOMES_AT + (at >> 1)] = jnp.where(there, home, 0)
        return 0

    lax.fori_loop(0, devices, place, 0, unroll=4)
    plan[PAIRS_AT] = n >> 1

    def expand(i, _):
        for j in range(2 * PAIR_UNROLL):
            at = i * 2 * PAIR_UNROLL + j
            item = plan[at]
            row = jnp.maximum(item, 0)
            packed = box[pl.ds((row >> 1) * ROWS + SHARE_ROW + (row & 1) * (S // 2), S // 2), :]
            unit = jnp.where(item < 0, 0.0, 1.0 / M_SCALE)
            shares[pl.ds(S * at, S), :] = (
                jnp.concatenate([upper(packed), lower(packed)], axis=0) * unit
            )
        return 0

    lax.fori_loop(0, jnp.maximum(pl.cdiv(n, 2 * PAIR_UNROLL), 1), expand, 0)


def advance(pos, vel, noise, word, top):
    wind = word * (1.0 / W_SCALE) - W_TOP
    fresh = DECAY * vel + KICK * noise
    return fresh, jnp.clip(pos + STEP * (wind + fresh), 0.0, top)


def take_up(places, box, z_rows):
    def take(b, _):
        z_rows[pl.ds(b, 1), :] = lax.shift_right_logical(
            box[pl.ds(places[3, b], 1), :], jnp.full((1, BLK), places[4, b], jnp.int32)
        )
        return 0

    lax.fori_loop(0, z_rows.shape[0], take, 0, unroll=8)
    return lower(z_rows[...])


def height_kernel(places, plan, box, pos, vel, noise, keys, out):
    def put(b, _):
        row = pl.ds(b, 1)
        word = lax.shift_right_logical(
            box[pl.ds(places[3, b], 1), :], jnp.full((1, BLK), places[4, b], jnp.int32)
        )
        _, height = advance(pos[2, row], vel[2, row], noise[2, row], lower(word), LEV - 1.0)
        out[pl.ds(places[5, b], 1), :] = (keys[row, :] << 16) | fixed(height, LEV_SCALE)
        return 0

    lax.fori_loop(0, keys.shape[0], put, 0, unroll=16)


def move_kernel(places, box, pos, vel, noise, moved, turb, yx_rows, z_rows):
    def take(b, _):
        yx_rows[pl.ds(b, 1), :] = box[pl.ds(places[2, b], 1), :]
        return 0

    lax.fori_loop(0, yx_rows.shape[0], take, 0, unroll=8)
    yx = yx_rows[...]
    words = (upper(yx), lower(yx), take_up(places, box, z_rows))
    for c, top in enumerate((BY - 1.0, BX - 1.0, LEV - 1.0)):
        turb[c], moved[c] = advance(pos[c], vel[c], noise[c], words[c], top)


def deposit_kernel(plan, box, shares, out, total, sems):
    n = plan[PAIRS_AT]
    total[...] = jnp.zeros(total.shape, jnp.float32)
    level = lax.broadcasted_iota(jnp.int32, (8, BLK), 0).astype(jnp.float32)
    cells = lax.broadcasted_iota(jnp.int32, (MBC, BLK), 0).astype(jnp.float32)
    cells = cells.astype(jnp.bfloat16)
    one, none = jnp.bfloat16(1), jnp.bfloat16(0)

    def step(first, length, done):
        for j in range(length):
            pair = first + j
            weights, picks = [], []
            for half in range(2):
                at = 2 * pair + half
                row = jnp.maximum(plan[at], 0)
                word = box[pl.ds(row, 1), :]
                height = jnp.broadcast_to(lower(word) * (1.0 / LEV_SCALE), (8, BLK))
                vert = [hat(height - (level + 8.0 * k)) for k in range(LEV // 8)]
                held = [
                    shares[pl.ds(S * at + s, 8, stride=0), :] * part for s in range(S) for part in vert
                ]
                weights.append(jnp.concatenate(held, axis=0).astype(jnp.bfloat16))
                cell = (word >> 16) & (MBC - 1)
                cell = cell.astype(jnp.float32).astype(jnp.bfloat16)
                picks.append(jnp.where(cells == cell, one, none))
            part = lax.dot_general(
                jnp.concatenate(weights, axis=1),
                jnp.concatenate(picks, axis=1),
                (((1,), (1,)), ((), ())),
                preferred_element_type=jnp.float32,
            )
            home = plan[HOMES_AT + pair]
            total[home] = total[home] + part
        later = first + length
        final = jnp.where(later < n, plan[HOMES_AT + later], MB)

        def leave(h, _):
            pltpu.make_async_copy(total.at[h], out.at[h], sems.at[h]).start()
            return 0

        lax.fori_loop(done, final, leave, 0)
        return final

    steps = (n + PAIR_UNROLL // 2 - 1) // PAIR_UNROLL
    done = lax.fori_loop(
        0, steps, lambda i, done: step(i * PAIR_UNROLL, PAIR_UNROLL, done), jnp.int32(0)
    )
    start = steps * PAIR_UNROLL
    short = jnp.maximum(pl.cdiv(n - start, PAIR_TAIL), jnp.where(steps == 0, 1, 0))
    lax.fori_loop(0, short, lambda i, done: step(start + i * PAIR_TAIL, PAIR_TAIL, done), done)
    for h in range(MB):
        pltpu.make_async_copy(total.at[h], out.at[h], sems.at[h]).wait()


def swap(box, devices):
    rows = box.shape[0] // devices
    step = 8 if rows % 8 == 0 else 2 if rows % 2 == 0 else 1
    whole_box = box.reshape(devices * rows // step, step, BLK)
    arrived = lax.all_to_all(whole_box, AXES, split_axis=0, concat_axis=0, tiled=True)
    return arrived.reshape(box.shape)


def body(
    winds, positions, velocity, increments, mass, requests, block_slots, destinations, cell_keys
):
    devices = lax.axis_size("lat") * lax.axis_size("lon")
    blocks = positions.shape[0]
    params = pltpu.CompilerParams(vmem_limit_bytes=40 << 20)
    smem, vmem, hbm = whole(pltpu.SMEM), whole(), whole(pltpu.HBM)
    i32, f32 = jnp.int32, jnp.float32
    dma = pltpu.SemaphoreType.DMA
    notes = [pltpu.VMEM((8, devices), i32), pltpu.SMEM((8, devices), i32)]
    by_part = (1, 0, 2)
    pos = positions.transpose(by_part)
    stay = lambda x: pltpu.with_memory_space_constraint(x, pltpu.HBM)
    others = lax.ppermute(winds, "lat", [(i, i ^ 1) for i in range(lax.axis_size("lat"))])
    both = jnp.stack([winds, others]).reshape(2 * MB, 3 * LEV, MBC)
    box, places = pl.pallas_call(
        pack_kernel,
        name="pack",
        out_shape=(
            jax.ShapeDtypeStruct((devices * ROWS, BLK), i32),
            jax.ShapeDtypeStruct((8, blocks), i32),
        ),
        in_specs=[hbm] * 6,
        out_specs=(vmem, smem),
        scratch_shapes=[
            pltpu.VMEM((1, blocks), i32),
            pltpu.VMEM((Q, devices), i32),
            pltpu.VMEM((1, blocks), i32),
            pltpu.VMEM((blocks, BLK), i32),
            pltpu.VMEM((3, blocks, BLK), f32),
            pltpu.VMEM((blocks, S, BLK), f32),
            pltpu.VMEM((blocks, BLK), i32),
            pltpu.VMEM((blocks, BLK), i32),
            pltpu.VMEM((devices * ROOM, BLK), i32),
            pltpu.VMEM((8, blocks), i32),
            dma((7,)),
        ],
        compiler_params=params,
    )(
        stay(block_slots.transpose(1, 0)),
        stay(requests.reshape(devices, Q).transpose(1, 0)),
        stay(destinations.transpose(1, 0)),
        stay(cell_keys),
        stay(pos),
        stay(mass),
    )
    box = swap(box, devices)
    local_wind = pl.pallas_call(
        sample_kernel,
        name="sample",
        out_shape=jax.ShapeDtypeStruct((devices * WIND_ROWS, BLK), i32),
        in_specs=[vmem] * 2,
        out_specs=vmem,
        scratch_shapes=[
            pltpu.SMEM((devices * ROOM + ROOM,), i32),
            pltpu.VMEM((devices * 2 * ROOM, BLK), i32),
            *notes,
            dma,
        ],
        compiler_params=params,
    )(box, both)
    room = devices * CAP + MB + 2 * PAIR_UNROLL
    assert room + devices * CAP <= HOMES_AT and HOMES_AT + (room + devices * CAP) // 2 < PAIRS_AT
    plan, shares = pl.pallas_call(
        order_kernel,
        name="order",
        cost_estimate=pl.CostEstimate(flops=10**9, bytes_accessed=20 << 20, transcendentals=0),
        out_shape=(
            jax.ShapeDtypeStruct((PLAN,), i32),
            jax.ShapeDtypeStruct((room * S, BLK), f32),
        ),
        in_specs=[vmem],
        out_specs=(smem, vmem),
        scratch_shapes=[
            *notes,
            pltpu.SMEM((MB + 1,), i32),
            pltpu.SMEM((MB + 1,), i32),
            dma,
        ],
        compiler_params=params,
    )(box)
    returned = swap(local_wind, devices)
    drift = (pos, velocity.transpose(by_part), increments.transpose(by_part))
    row_scratch = pltpu.VMEM((blocks, BLK), i32)
    outbox = pl.pallas_call(
        height_kernel,
        name="height",
        out_shape=jax.ShapeDtypeStruct((devices * CAP, BLK), i32),
        in_specs=[smem, whole(pl.ANY)] + [vmem] * 5,
        out_specs=vmem,
        compiler_params=params,
    )(
        places,
        plan,
        returned,
        *drift,
        cell_keys,
    )
    inbox = swap(outbox, devices)
    moved, turbulence = pl.pallas_call(
        move_kernel,
        name="move",
        out_shape=[jax.ShapeDtypeStruct(pos.shape, f32)] * 2,
        in_specs=[smem] + [vmem] * 4,
        out_specs=[vmem] * 2,
        scratch_shapes=[row_scratch, row_scratch],
        cost_estimate=pl.CostEstimate(flops=10**7, bytes_accessed=2 << 20, transcendentals=0),
        compiler_params=params,
    )(places, returned, *drift)
    total = pl.pallas_call(
        deposit_kernel,
        name="deposit",
        out_shape=jax.ShapeDtypeStruct((MB, S * LEV, MBC), f32),
        in_specs=[smem, vmem, vmem],
        out_specs=hbm,
        scratch_shapes=[pltpu.VMEM((MB, S * LEV, MBC), f32), dma((MB,))],
        compiler_params=params,
    )(plan, inbox, shares)
    return (
        moved.transpose(by_part),
        turbulence.transpose(by_part),
        total.reshape(winds.shape[:2] + (S, LEV, MBC)),
    )


def solution(mesh):
    rows = P(AXES, None, None)
    pairs = P(AXES, None)
    tiles = P("lat", "lon", None, None, None)
    return jax.shard_map(
        body,
        mesh=mesh,
        in_specs=(tiles, rows, rows, rows, rows, rows, pairs, pairs, pairs),
        out_specs=(rows, rows, tiles),
        check_vma=False,
    )
```

```python
import jax
import jax.numpy as jnp
from jax import lax
from jax.experimental import pallas as pl
from jax.experimental.pallas import tpu as pltpu
from jax.sharding import PartitionSpec as P

BY = 8
BX = 16
MBC = 128
LEV = 40
S = 8
BLK = 128
MB = 16
Q = 2
CAP = 2
ROOM = Q * CAP

DECAY = 0.8
KICK = 0.6
STEP = 0.5

AXES = ("lat", "lon")
LOW16 = 0xFFFF
ROW_SCALE = 65535.0 / (BY - 1)
COL_SCALE = 65535.0 / (BX - 1)
LEV_SCALE = 65535.0 / (LEV - 1)
Z_SCALE = float((1 << 20) - 1) / (LEV - 1)
W_TOP = 6.1
W_SCALE = 65535.0 / (2 * W_TOP)
M_SCALE = 32767.0
SAMPLE_UNROLL = 12
PAIR_UNROLL = 16
PAIR_TAIL = 4

HIGH_ROW = ROOM
NOTE_ROW = HIGH_ROW + ROOM // 2
SHARE_ROW = NOTE_ROW + 1
ROWS = SHARE_ROW + CAP * S // 2
WIND_ROWS = ROOM + ROOM // 2
HOME_AT = ROOM
LANDED_AT = HOME_AT + CAP
TAKEN_AT = LANDED_AT + 1
EACH = 8
PLAN = 1024
HOMES_AT = 576
PAIRS_AT = PLAN - 1


def hat(offset):
    return jnp.maximum(0.0, 1.0 - jnp.abs(offset))


def fixed(value, scale, shift=0.0):
    return ((value + shift) * scale + 0.5).astype(jnp.int32)


def upper(word):
    return lax.shift_right_logical(word, jnp.int32(16)).astype(jnp.float32)


def lower(word):
    return (word & LOW16).astype(jnp.float32)


def whole(space=pltpu.VMEM):
    return pl.BlockSpec(memory_space=space)


def read_notes(box, rows, notes, sem):
    devices = notes.shape[1]
    sent = upper(box[pl.ds(NOTE_ROW, devices, stride=ROWS), :])
    rows[...] = sent.T[0 : notes.shape[0], :].astype(jnp.int32)
    copy = pltpu.make_async_copy(rows, notes, sem)
    copy.start()
    copy.wait()


def pack_kernel(
    slots_hbm, asked_hbm, targets_hbm, keys_hbm, pos_hbm, mass_hbm,
    box, places,
    slots, asked, targets, keys, pos, mass, yx_rows, z_rows, heights, ranks, sems,
):
    blocks, devices = mass.shape[0], asked.shape[1]
    copies = [
        pltpu.make_async_copy(src, dst, sems.at[i])
        for i, (src, dst) in enumerate(
            (
                (slots_hbm, slots),
                (targets_hbm, targets),
                (asked_hbm, asked),
                (keys_hbm, keys),
                (pos_hbm, pos),
                (mass_hbm, mass),
            )
        )
    ]
    for copy in copies:
        copy.start()
    square = (blocks, blocks)
    down = lax.broadcasted_iota(jnp.int32, square, 0)
    along = lax.broadcasted_iota(jnp.int32, square, 1)

    def stand(row):
        return jnp.broadcast_to(row.astype(jnp.float32), square).T.astype(jnp.int32)

    def rank(row):
        same = (stand(row) == row) & (down < along)
        return jnp.sum(jnp.where(same, 1.0, 0.0), axis=0, keepdims=True).astype(jnp.int32)

    copies[0].wait()
    slot = slots[...]
    tile = slot >> 1
    order = rank(tile)
    lons = lax.axis_size("lon")
    core = (tile >> (lons.bit_length() - 1)) & 1
    helper = (order + lax.axis_index("lat") + lax.axis_index("lon")) & 1
    host = tile + (helper - core) * lons
    seat = core * (ROOM // 2) + (order >> 1)
    copies[1].wait()
    target = targets[...]
    turn = rank(target)
    ranks[0:1, :] = host * ROWS + seat
    ranks[1:2, :] = target * ROWS + SHARE_ROW + turn * (S // 2)
    ranks[2:3, :] = host * WIND_ROWS + seat
    ranks[3:4, :] = host * WIND_ROWS + ROOM + (seat >> 1)
    ranks[4:5, :] = 16 - 16 * (seat & 1)
    ranks[5:6, :] = target * CAP + turn
    ranks[6:7, :] = host * ROOM + seat
    ranked = pltpu.make_async_copy(ranks, places, sems.at[len(copies)])
    ranked.start()
    bits = stand((turn << 15) | (seat << 13) | (helper << 12) | slot)
    slot_down = bits & 0xFFF
    helper_down = (bits >> 12) & 1
    seat_down = (bits >> 13) & (ROOM - 1)
    turn_down = bits >> 15
    core_down = seat_down >> 1
    copies[2].wait()
    met = jnp.where((slot_down & 1) == 0, asked[0:1, :], asked[1:2, :])
    met = jnp.where((slot_down >> 1) == along, met, 0).astype(jnp.float32)
    met = jnp.sum(met, axis=1, keepdims=True)
    met = met + jnp.where(helper_down == core_down, 0.0, float(MB))
    copies[3].wait()
    home = (keys[:, 0:1] >> 7).astype(jnp.float32)
    said = jnp.where(along == seat_down, met, 0.0)
    said = jnp.where(along == TAKEN_AT, jnp.where(core_down == 0, 1.0, float(EACH)), said)
    more = jnp.where(along == HOME_AT + turn_down, home, 0.0) + jnp.where(
        along == LANDED_AT, 1.0, 0.0
    )
    mine = jnp.concatenate([down == host, down == target], axis=1)
    notes = jnp.dot(
        jnp.where(mine, 1.0, 0.0).astype(jnp.bfloat16),
        jnp.concatenate([said, more], axis=0).astype(jnp.bfloat16),
        preferred_element_type=jnp.float32,
    )
    copies[4].wait()
    yx_rows[...] = (fixed(pos[0], ROW_SCALE) << 16) | fixed(pos[1], COL_SCALE)
    z_rows[...] = fixed(pos[2], Z_SCALE)
    copies[5].wait()
    ranked.wait()

    def put(b, _):
        box[pl.ds(places[0, b], 1), :] = yx_rows[pl.ds(b, 1), :]
        heights[pl.ds(places[6, b], 1), :] = z_rows[pl.ds(b, 1), :]
        share = fixed(mass[b], M_SCALE)
        box[pl.ds(places[1, b], S // 2), :] = (share[0 : S // 2] << 16) | share[S // 2 :]
        return 0

    lax.fori_loop(0, blocks, put, 0, unroll=32)
    each = [heights[pl.ds(k, devices, stride=ROOM), :] for k in range(ROOM)]
    for k in range(0, ROOM, 2):
        box[pl.ds(HIGH_ROW + k // 2, devices, stride=ROWS), :] = ((each[k] >> 4) << 16) | (
            (each[k + 1] >> 4) & LOW16
        )
    word = notes.astype(jnp.int32) << 16
    for k in range(ROOM):
        word = word | ((each[k] & 15) << (12 - 4 * k))
    box[pl.ds(NOTE_ROW, devices, stride=ROWS), :] = word


def sample_kernel(box, winds, out, queue, found, rows, notes, sem):
    devices = notes.shape[1]
    read_notes(box, rows, notes, sem)

    def enlist(t, n):
        taken = notes[TAKEN_AT, t]
        for r in range(ROOM // 2):
            queue[n + r] = t * ROOM + r
        n = n + (taken & (EACH - 1))
        for r in range(ROOM // 2):
            queue[n + r] = t * ROOM + ROOM // 2 + r
        return n + (taken >> 3)

    n = lax.fori_loop(0, devices, enlist, 0, unroll=4)
    levels = lax.broadcasted_iota(jnp.int32, (LEV, BLK), 0).astype(jnp.float32)
    lats = lax.broadcasted_iota(jnp.int32, (BY, BLK), 0).astype(jnp.float32)
    lons = lax.broadcasted_iota(jnp.int32, (BX, BLK), 0).astype(jnp.float32)

    def step(i, _):
        for j in range(SAMPLE_UNROLL):
            item = queue[jnp.minimum(i * SAMPLE_UNROLL + j, n - 1)]
            src, seat = item >> 2, item & (ROOM - 1)
            row = src * ROWS
            yx = box[pl.ds(row + seat, 1), :]
            high = lax.shift_right_logical(
                box[pl.ds(row + HIGH_ROW + (seat >> 1), 1), :],
                jnp.full((1, BLK), 16 - 16 * (seat & 1), jnp.int32),
            )
            low = box[pl.ds(row + NOTE_ROW, 1), :] >> jnp.full((1, BLK), 12 - 4 * seat, jnp.int32)
            height = ((high & LOW16) << 4) | (low & 15)
            hy = hat(upper(yx) * (1.0 / ROW_SCALE) - lats)
            hx = hat(lower(yx) * (1.0 / COL_SCALE) - lons)
            wz = hat(height.astype(jnp.float32) * (1.0 / Z_SCALE) - levels)
            wz = wz.astype(jnp.bfloat16).astype(jnp.float32)
            flat = (hy[:, None, :] * hx[None, :, :]).reshape(MBC, BLK)
            high = flat.astype(jnp.bfloat16)
            low = (flat - high.astype(jnp.float32)).astype(jnp.bfloat16)
            met = winds[notes[seat, src]]
            level_wind = jnp.dot(met, high, preferred_element_type=jnp.float32) + jnp.dot(
                met, low, preferred_element_type=jnp.float32
            )
            wind = [
                jnp.sum(level_wind[c * LEV : (c + 1) * LEV] * wz, axis=0, keepdims=True)
                for c in range(3)
            ]
            found[pl.ds(2 * item, 1), :] = (fixed(wind[0], W_SCALE, W_TOP) << 16) | fixed(
                wind[1], W_SCALE, W_TOP
            )
            found[pl.ds(2 * item + 1, 1), :] = fixed(wind[2], W_SCALE, W_TOP)
        return 0

    lax.fori_loop(0, pl.cdiv(n, SAMPLE_UNROLL), step, 0)

    def every(r):
        return found[pl.ds(r, devices, stride=2 * ROOM), :]

    for r in range(ROOM):
        out[pl.ds(r, devices, stride=WIND_ROWS), :] = every(2 * r)
    for r in range(0, ROOM, 2):
        out[pl.ds(ROOM + r // 2, devices, stride=WIND_ROWS), :] = (every(2 * r + 1) << 16) | (
            every(2 * r + 3) & LOW16
        )


def order_kernel(box, plan, shares, rows, notes, starts, tally, sem):
    devices = notes.shape[1]
    read_notes(box, rows, notes, sem)

    room = shares.shape[0] // S

    def clear(i, _):
        plan[i] = -1
        return 0

    lax.fori_loop(0, room, clear, 0, unroll=8)

    def clear_home(i, _):
        plan[HOMES_AT + i] = 0
        return 0

    lax.fori_loop(0, room // 2, clear_home, 0, unroll=8)
    for h in range(MB):
        tally[h] = 0

    def tell(t, _):
        landed = notes[LANDED_AT, t]
        for r in range(CAP):
            home = jnp.where(r < landed, notes[HOME_AT + r, t], MB)
            tally[home] = tally[home] + 1
        return 0

    tally[MB] = 0
    lax.fori_loop(0, devices, tell, 0, unroll=4)
    n = jnp.int32(0)
    for h in range(MB):
        starts[h] = n
        n = n + ((tally[h] + 1) & ~1)
    starts[MB] = room

    def place(t, _):
        landed = notes[LANDED_AT, t]
        for r in range(CAP):
            there = r < landed
            home = jnp.where(there, notes[HOME_AT + r, t], MB)
            at = starts[home]
            starts[home] = at + 1
            plan[at] = jnp.where(there, t * CAP + r, -1)
            plan[HOMES_AT + (at >> 1)] = jnp.where(there, home, 0)
        return 0

    lax.fori_loop(0, devices, place, 0, unroll=4)
    plan[PAIRS_AT] = n >> 1

    def expand(i, _):
        for j in range(2 * PAIR_UNROLL):
            at = i * 2 * PAIR_UNROLL + j
            item = plan[at]
            row = jnp.maximum(item, 0)
            packed = box[pl.ds((row >> 1) * ROWS + SHARE_ROW + (row & 1) * (S // 2), S // 2), :]
            unit = jnp.where(item < 0, 0.0, 1.0 / M_SCALE)
            shares[pl.ds(S * at, S), :] = (
                jnp.concatenate([upper(packed), lower(packed)], axis=0) * unit
            )
        return 0

    lax.fori_loop(0, jnp.maximum(pl.cdiv(n, 2 * PAIR_UNROLL), 1), expand, 0)


def advance(pos, vel, noise, word, top):
    wind = word * (1.0 / W_SCALE) - W_TOP
    fresh = DECAY * vel + KICK * noise
    return fresh, jnp.clip(pos + STEP * (wind + fresh), 0.0, top)


def take_up(places, box, z_rows):
    def take(b, _):
        z_rows[pl.ds(b, 1), :] = lax.shift_right_logical(
            box[pl.ds(places[3, b], 1), :], jnp.full((1, BLK), places[4, b], jnp.int32)
        )
        return 0

    lax.fori_loop(0, z_rows.shape[0], take, 0, unroll=8)
    return lower(z_rows[...])


def height_kernel(places, plan, box, pos, vel, noise, keys, out):
    def put(b, _):
        row = pl.ds(b, 1)
        word = lax.shift_right_logical(
            box[pl.ds(places[3, b], 1), :], jnp.full((1, BLK), places[4, b], jnp.int32)
        )
        _, height = advance(pos[2, row], vel[2, row], noise[2, row], lower(word), LEV - 1.0)
        out[pl.ds(places[5, b], 1), :] = (keys[row, :] << 16) | fixed(height, LEV_SCALE)
        return 0

    lax.fori_loop(0, keys.shape[0], put, 0, unroll=32)


def move_kernel(places, box, pos, vel, noise, moved, turb, yx_rows, z_rows):
    def take(b, _):
        yx_rows[pl.ds(b, 1), :] = box[pl.ds(places[2, b], 1), :]
        return 0

    lax.fori_loop(0, yx_rows.shape[0], take, 0, unroll=8)
    yx = yx_rows[...]
    words = (upper(yx), lower(yx), take_up(places, box, z_rows))
    for c, top in enumerate((BY - 1.0, BX - 1.0, LEV - 1.0)):
        turb[c], moved[c] = advance(pos[c], vel[c], noise[c], words[c], top)


def deposit_kernel(plan, box, shares, out, total, sems):
    n = plan[PAIRS_AT]
    total[...] = jnp.zeros(total.shape, jnp.float32)
    level = lax.broadcasted_iota(jnp.int32, (8, BLK), 0).astype(jnp.float32)
    cells = lax.broadcasted_iota(jnp.int32, (MBC, BLK), 0).astype(jnp.float32)
    cells = cells.astype(jnp.bfloat16)
    one, none = jnp.bfloat16(1), jnp.bfloat16(0)

    def step(first, length, done):
        for j in range(length):
            pair = first + j
            weights, picks = [], []
            for half in range(2):
                at = 2 * pair + half
                row = jnp.maximum(plan[at], 0)
                word = box[pl.ds(row, 1), :]
                height = jnp.broadcast_to(lower(word) * (1.0 / LEV_SCALE), (8, BLK))
                vert = [hat(height - (level + 8.0 * k)) for k in range(LEV // 8)]
                held = [
                    shares[pl.ds(S * at + s, 8, stride=0), :] * part for s in range(S) for part in vert
                ]
                weights.append(jnp.concatenate(held, axis=0).astype(jnp.bfloat16))
                cell = (word >> 16) & (MBC - 1)
                cell = cell.astype(jnp.float32).astype(jnp.bfloat16)
                picks.append(jnp.where(cells == cell, one, none))
            part = lax.dot_general(
                jnp.concatenate(weights, axis=1),
                jnp.concatenate(picks, axis=1),
                (((1,), (1,)), ((), ())),
                preferred_element_type=jnp.float32,
            )
            home = plan[HOMES_AT + pair]
            total[home] = total[home] + part
        later = first + length
        final = jnp.where(later < n, plan[HOMES_AT + later], MB)

        def leave(h, _):
            pltpu.make_async_copy(total.at[h], out.at[h], sems.at[h]).start()
            return 0

        lax.fori_loop(done, final, leave, 0)
        return final

    steps = (n + PAIR_UNROLL // 2 - 1) // PAIR_UNROLL
    done = lax.fori_loop(
        0, steps, lambda i, done: step(i * PAIR_UNROLL, PAIR_UNROLL, done), jnp.int32(0)
    )
    start = steps * PAIR_UNROLL
    short = jnp.maximum(pl.cdiv(n - start, PAIR_TAIL), jnp.where(steps == 0, 1, 0))
    lax.fori_loop(0, short, lambda i, done: step(start + i * PAIR_TAIL, PAIR_TAIL, done), done)
    for h in range(MB):
        pltpu.make_async_copy(total.at[h], out.at[h], sems.at[h]).wait()


def swap(box, devices):
    rows = box.shape[0] // devices
    step = 8 if rows % 8 == 0 else 2 if rows % 2 == 0 else 1
    whole_box = box.reshape(devices * rows // step, step, BLK)
    arrived = lax.all_to_all(whole_box, AXES, split_axis=0, concat_axis=0, tiled=True)
    return arrived.reshape(box.shape)


def body(
    winds, positions, velocity, increments, mass, requests, block_slots, destinations, cell_keys
):
    devices = lax.axis_size("lat") * lax.axis_size("lon")
    blocks = positions.shape[0]
    params = pltpu.CompilerParams(vmem_limit_bytes=40 << 20)
    smem, vmem, hbm = whole(pltpu.SMEM), whole(), whole(pltpu.HBM)
    i32, f32 = jnp.int32, jnp.float32
    dma = pltpu.SemaphoreType.DMA
    notes = [pltpu.VMEM((8, devices), i32), pltpu.SMEM((8, devices), i32)]
    by_part = (1, 0, 2)
    pos = positions.transpose(by_part)
    stay = lambda x: pltpu.with_memory_space_constraint(x, pltpu.HBM)
    others = lax.ppermute(winds, "lat", [(i, i ^ 1) for i in range(lax.axis_size("lat"))])
    both = jnp.stack([winds, others]).reshape(2 * MB, 3 * LEV, MBC)
    box, places = pl.pallas_call(
        pack_kernel,
        name="pack",
        out_shape=(
            jax.ShapeDtypeStruct((devices * ROWS, BLK), i32),
            jax.ShapeDtypeStruct((8, blocks), i32),
        ),
        in_specs=[hbm] * 6,
        out_specs=(vmem, smem),
        scratch_shapes=[
            pltpu.VMEM((1, blocks), i32),
            pltpu.VMEM((Q, devices), i32),
            pltpu.VMEM((1, blocks), i32),
            pltpu.VMEM((blocks, BLK), i32),
            pltpu.VMEM((3, blocks, BLK), f32),
            pltpu.VMEM((blocks, S, BLK), f32),
            pltpu.VMEM((blocks, BLK), i32),
            pltpu.VMEM((blocks, BLK), i32),
            pltpu.VMEM((devices * ROOM, BLK), i32),
            pltpu.VMEM((8, blocks), i32),
            dma((7,)),
        ],
        compiler_params=params,
    )(
        stay(block_slots.transpose(1, 0)),
        stay(requests.reshape(devices, Q).transpose(1, 0)),
        stay(destinations.transpose(1, 0)),
        stay(cell_keys),
        stay(pos),
        stay(mass),
    )
    box = swap(box, devices)
    local_wind = pl.pallas_call(
        sample_kernel,
        name="sample",
        out_shape=jax.ShapeDtypeStruct((devices * WIND_ROWS, BLK), i32),
        in_specs=[vmem] * 2,
        out_specs=vmem,
        scratch_shapes=[
            pltpu.SMEM((devices * ROOM + ROOM,), i32),
            pltpu.VMEM((devices * 2 * ROOM, BLK), i32),
            *notes,
            dma,
        ],
        compiler_params=params,
    )(box, both)
    room = devices * CAP + MB + 2 * PAIR_UNROLL
    assert room + devices * CAP <= HOMES_AT and HOMES_AT + (room + devices * CAP) // 2 < PAIRS_AT
    plan, shares = pl.pallas_call(
        order_kernel,
        name="order",
        cost_estimate=pl.CostEstimate(flops=10**9, bytes_accessed=20 << 20, transcendentals=0),
        out_shape=(
            jax.ShapeDtypeStruct((PLAN,), i32),
            jax.ShapeDtypeStruct((room * S, BLK), f32),
        ),
        in_specs=[vmem],
        out_specs=(smem, vmem),
        scratch_shapes=[
            *notes,
            pltpu.SMEM((MB + 1,), i32),
            pltpu.SMEM((MB + 1,), i32),
            dma,
        ],
        compiler_params=params,
    )(box)
    returned = swap(local_wind, devices)
    drift = (pos, velocity.transpose(by_part), increments.transpose(by_part))
    row_scratch = pltpu.VMEM((blocks, BLK), i32)
    outbox = pl.pallas_call(
        height_kernel,
        name="height",
        out_shape=jax.ShapeDtypeStruct((devices * CAP, BLK), i32),
        in_specs=[smem, whole(pl.ANY)] + [vmem] * 5,
        out_specs=vmem,
        compiler_params=params,
    )(
        places,
        plan,
        returned,
        *drift,
        cell_keys,
    )
    inbox = swap(outbox, devices)
    moved, turbulence = pl.pallas_call(
        move_kernel,
        name="move",
        out_shape=[jax.ShapeDtypeStruct(pos.shape, f32)] * 2,
        in_specs=[smem] + [vmem] * 4,
        out_specs=[vmem] * 2,
        scratch_shapes=[row_scratch, row_scratch],
        cost_estimate=pl.CostEstimate(flops=10**7, bytes_accessed=2 << 20, transcendentals=0),
        compiler_params=params,
    )(places, returned, *drift)
    total = pl.pallas_call(
        deposit_kernel,
        name="deposit",
        out_shape=jax.ShapeDtypeStruct((MB, S * LEV, MBC), f32),
        in_specs=[smem, vmem, vmem],
        out_specs=hbm,
        scratch_shapes=[pltpu.VMEM((MB, S * LEV, MBC), f32), dma((MB,))],
        compiler_params=params,
    )(plan, inbox, shares)
    return (
        moved.transpose(by_part),
        turbulence.transpose(by_part),
        total.reshape(winds.shape[:2] + (S, LEV, MBC)),
    )


def solution(mesh):
    rows = P(AXES, None, None)
    pairs = P(AXES, None)
    tiles = P("lat", "lon", None, None, None)
    return jax.shard_map(
        body,
        mesh=mesh,
        in_specs=(tiles, rows, rows, rows, rows, rows, pairs, pairs, pairs),
        out_specs=(rows, rows, tiles),
        check_vma=False,
    )
```
